32 devices in a mesh: grp: 2 (over y), sp: 4 (over x, core), ch: 4 (over z).
Axes of the slice: x: 2, y: 2, z: 4, core: 2. Of those that a mesh axis runs over, the one named last changes fastest.
Arguments:
- flow: float32 [4, 64, 64, 256], P(None, ('grp', 'sp'), 'ch'), may hold values from -6 to 6
- embed_w: bfloat16 [2048, 512], P(None, 'ch'), may hold values from -0.125 to 0.125
- conv_w: bfloat16 [2, 27, 512, 512], P(None, None, None, 'ch'), may hold values from -0.109375 to 0.109375
- dec_w: bfloat16 [512, 2048], P(None, 'ch'), may hold values from -0.25 to 0.25
- conv_m: float32 [2, 27, 512, 512], P(None, None, ('grp', 'sp'), 'ch'), may hold values from -0.00018 to 0.00018
- conv_v: float32 [2, 27, 512, 512], P(None, None, ('grp', 'sp'), 'ch'), may hold values from 1e-10 to 1e-07
- dec_m: float32 [512, 2048], P(('grp', 'sp'), 'ch'), may hold values from -0.0006 to 0.0006
- dec_v: float32 [512, 2048], P(('grp', 'sp'), 'ch'), may hold values from 1e-09 to 1e-06
- loss_mask: int32 [8, 8, 32], P(('grp', 'sp')), may hold values 0 or 1
Outputs:
- flow_next: float32 [4, 64, 64, 256], P(None, ('grp', 'sp'), 'ch')
- loss: float32 [], replicated
- conv_w_next: bfloat16 [2, 27, 512, 512], P(None, None, None, 'ch')
- dec_w_next: bfloat16 [512, 2048], P(None, 'ch')
- conv_m_next: float32 [2, 27, 512, 512], P(None, None, ('grp', 'sp'), 'ch')
- conv_v_next: float32 [2, 27, 512, 512], P(None, None, ('grp', 'sp'), 'ch')
- dec_m_next: float32 [512, 2048], P(('grp', 'sp'), 'ch')
- dec_v_next: float32 [512, 2048], P(('grp', 'sp'), 'ch')
The draws below stay inside these ranges and needn't reach their ends.
All inputs are finite; a program needn't handle non-finite values. No bound on the sum of `loss_mask` on one device may be relied on, other than what follows from the above.
Results may differ from the reference program's by a relative error of at most 0.01.
Values may be sent and summed in bfloat16 or wider, within the bound.
No kernel may reach another device: no remote copies, remote signals or barrier semaphores. Data moves between devices by JAX's collectives and lax.ppermute only.
A program may use at most 192 MiB of HBM per device.

```python
import math
import jax
import jax.numpy as jnp
from jax import lax

FIELDS = 4
PATCH = 8
WIDTH = 512
TAPS = 27
FLOW_STEPS = 2
NZ = 256
OUT = 2048
NX = 64
NY = 64
NPX = 8
NPY = 8
NPZ = 32


def plant(drawn, own_key, low, top_value):
    shape = drawn.shape
    spot = [jax.random.randint(jax.random.fold_in(own_key, axis), (), 0, shape[axis]) for axis in range(len(shape))]
    drawn = drawn.at[tuple(spot)].set(low)
    longest = shape.index(max(shape))
    spot[longest] = (spot[longest] + 1) % shape[longest]
    return drawn.at[tuple(spot)].set(top_value)


def level_of(rng, extent, shards, least, largest):
    level, own = 1.0, jax.random.fold_in(rng, 6)
    for axis_at, parts in shards:
        heights = jnp.exp(jax.random.uniform(jax.random.fold_in(own, axis_at), (parts,), jnp.float32, least / len(shards), largest / len(shards)))
        level = level * jnp.repeat(heights, extent[axis_at] // parts).reshape([-1 if axis == axis_at else 1 for axis in range(len(extent))])
    return level


def bell_draw(key, dims, deviation, bound, pieces=(), kind=jnp.bfloat16):
    factor_of = level_of(key, dims, pieces, -0.22, 0.18) if pieces else 1.0
    values = jax.random.normal(key, dims, jnp.float32) * deviation * factor_of
    return jnp.minimum(jnp.maximum(values, -bound), bound).astype(kind)


def setup_inputs(seed: int = 0) -> dict:
    key_of = jax.random.split(jax.random.key(seed), 10)
    return {
        "flow": bell_draw(key_of[0], (FIELDS, NX, NY, NZ), 1.0, 6.0, ((1, 8), (2, 4)), jnp.float32),
        "embed_w": bell_draw(key_of[1], (OUT, WIDTH), OUT ** -0.5, 0.125, ((1, 4),)),
        "conv_w": bell_draw(key_of[2], (2, TAPS, WIDTH, WIDTH), (TAPS * WIDTH // 4) ** -0.5, 0.109375, ((3, 4),)),
        "dec_w": bell_draw(key_of[3], (WIDTH, OUT), WIDTH ** -0.5, 0.25, ((1, 4),)),
        "conv_m": bell_draw(key_of[4], (2, TAPS, WIDTH, WIDTH), (3e-5), 0.00018, ((2, 8), (3, 4)), jnp.float32),
        "conv_v": jnp.clip(jnp.exp(math.log(1.0000000116860974e-07) - 6.9077553 * jax.random.uniform(key_of[5], (2, TAPS, WIDTH, WIDTH), jnp.float32) ** level_of(key_of[5], (2, TAPS, WIDTH, WIDTH), ((2, 8), (3, 4)), -0.2, 0.2)), 1.000000013351432e-10, 1.0000000116860974e-07),
        "dec_m": bell_draw(key_of[6], (WIDTH, OUT), (1e-4), 0.0006, ((0, 8), (1, 4)), jnp.float32),
        "dec_v": jnp.clip(jnp.exp(math.log(9.999999974752427e-07) - 6.9077553 * jax.random.uniform(key_of[7], (WIDTH, OUT), jnp.float32) ** level_of(key_of[7], (WIDTH, OUT), ((0, 8), (1, 4)), -0.2, 0.2)), 9.999999717180685e-10, 9.999999974752427e-07),
        "loss_mask": plant((jax.random.randint(key_of[8], (NPX, NPY, NPZ), 0, 4) < 3).astype(jnp.int32), jax.random.fold_in(key_of[8], 1), 0, 1),
    }


time_step = 0.1
viscosity = 0.2
beta_one = 0.9
beta_two = 0.95
learn_rate = 0.001
adam_eps = 1e-08
bias_one = 0.9999734386011124
bias_two = 0.994079470779666

def advance(field):
    east = jnp.roll(field, -1, 1)
    west = jnp.roll(field, 1, 1)
    north = jnp.roll(field, -1, 2)
    south = jnp.roll(field, 1, 2)
    upper = jnp.roll(field, -1, 3)
    lower = jnp.roll(field, 1, 3)
    laplace = east + west + north + south + upper + lower - 6.0 * field
    carried = field[0:1] * (east - west) * 0.5 + field[1:2] * (north - south) * 0.5 + field[2:3] * (upper - lower) * 0.5
    return field + time_step * (viscosity * laplace - carried)

def patchify(field):
    fields = field.shape[0]
    blocks = field.reshape(fields, NPX, PATCH, NPY, PATCH, NPZ, PATCH)
    return blocks.transpose(1, 3, 5, 0, 2, 4, 6).reshape(NPX * NPY * NPZ, fields * PATCH ** 3)

def tap_list():
    return [(plane, down, across) for plane in range(3) for down in (-1, 0, 1) for across in (-1, 0, 1)]

def convolve(act, kernel):
    cube = act.reshape(NPX, NPY, NPZ, -1)
    total = jnp.zeros((act.shape[0], kernel.shape[2]), jnp.float32)
    for index, (plane, down, across) in enumerate(tap_list()):
        shifted = jnp.roll(cube, (1 - plane, -down, -across), (0, 1, 2)).reshape(act.shape[0], -1)
        total = total + jnp.dot(shifted, kernel[index], preferred_element_type=jnp.float32)
    return total

def convolve_back(error, kernel):
    cube = error.reshape(NPX, NPY, NPZ, -1)
    total = jnp.zeros((error.shape[0], kernel.shape[1]), jnp.float32)
    for index, (plane, down, across) in enumerate(tap_list()):
        shifted = jnp.roll(cube, (plane - 1, down, across), (0, 1, 2)).reshape(error.shape[0], -1)
        total = total + lax.dot_general(shifted, kernel[index], (((1,), (1,)), ((), ())), preferred_element_type=jnp.float32)
    return total

def kernel_grad(act, error):
    cube = act.reshape(NPX, NPY, NPZ, -1)
    grads = []
    for plane, down, across in tap_list():
        shifted = jnp.roll(cube, (1 - plane, -down, -across), (0, 1, 2)).reshape(act.shape[0], -1)
        grads.append(lax.dot_general(shifted, error, (((0,), (0,)), ((), ())), preferred_element_type=jnp.float32))
    return jnp.stack(grads)

def silu_slope(value):
    sig = jax.nn.sigmoid(value)
    return sig * (1.0 + value * (1.0 - sig))

def adam(weight, moment, second, grad):
    moment_next = beta_one * moment + (1.0 - beta_one) * grad
    second_next = beta_two * second + (1.0 - beta_two) * grad * grad
    weight_next = weight.astype(jnp.float32) - learn_rate * (moment_next / bias_one) / (jnp.sqrt(second_next / bias_two) + adam_eps)
    return (weight_next.astype(jnp.bfloat16), moment_next, second_next)

def reference(flow, embed_w, conv_w, dec_w, conv_m, conv_v, dec_m, dec_v, loss_mask):
    state = flow
    for step in range(FLOW_STEPS):
        state = advance(state)
    patches_in = patchify(flow).astype(jnp.bfloat16)
    targets = patchify(state)
    embedded = jnp.dot(patches_in, embed_w, preferred_element_type=jnp.float32).astype(jnp.bfloat16)
    pre_one = convolve(embedded, conv_w[0])
    act_one = (embedded.astype(jnp.float32) + jax.nn.silu(pre_one)).astype(jnp.bfloat16)
    pre_two = convolve(act_one, conv_w[1])
    act_two = (act_one.astype(jnp.float32) + jax.nn.silu(pre_two)).astype(jnp.bfloat16)
    pred = patches_in.astype(jnp.float32) + jnp.dot(act_two, dec_w, preferred_element_type=jnp.float32)
    weights = loss_mask.reshape(-1).astype(jnp.float32)[:, None]
    resid = pred - targets
    denom = jnp.maximum(jnp.sum(weights), 1.0) * OUT
    loss = jnp.sum(weights * resid * resid) / denom
    d_pred = (2.0 * weights * resid / denom).astype(jnp.bfloat16)
    grad_dec = lax.dot_general(act_two, d_pred, (((0,), (0,)), ((), ())), preferred_element_type=jnp.float32)
    d_act_two = lax.dot_general(d_pred, dec_w, (((1,), (1,)), ((), ())), preferred_element_type=jnp.float32)
    d_pre_two = (d_act_two * silu_slope(pre_two)).astype(jnp.bfloat16)
    grad_two = kernel_grad(act_one, d_pre_two)
    d_act_one = d_act_two + convolve_back(d_pre_two, conv_w[1])
    d_pre_one = (d_act_one * silu_slope(pre_one)).astype(jnp.bfloat16)
    grad_one = kernel_grad(embedded, d_pre_one)
    conv_next, conv_m_next, conv_v_next = adam(conv_w, conv_m, conv_v, jnp.stack([grad_one, grad_two]))
    dec_next, dec_m_next, dec_v_next = adam(dec_w, dec_m, dec_v, grad_dec)
    return (state, loss, conv_next, dec_next, conv_m_next, conv_v_next, dec_m_next, dec_v_next)
```

```python
import jax
import jax.numpy as jnp
from jax import lax
from jax.experimental import pallas as pl
from jax.experimental.pallas import tpu as pltpu
from jax.sharding import PartitionSpec as P

PATCH = 8
FLOW_STEPS = 2
OUT = 2048
SPLIT = ("grp", "sp")


time_step = 0.1
viscosity = 0.2
beta_one = 0.9
beta_two = 0.95
learn_rate = 0.001
adam_eps = 1e-08
bias_one = 0.9999734386011124
bias_two = 0.994079470779666


def shift(block, axis, by):
    count = lax.axis_size(axis)
    return lax.ppermute(block, axis, [(i, (i + by) % count) for i in range(count)])


def with_halo(block, sides, width):
    for axis, dim in sides:
        low = shift(
            lax.slice_in_dim(block, block.shape[dim] - width, None, axis=dim), axis, 1
        )
        high = shift(lax.slice_in_dim(block, 0, width, axis=dim), axis, -1)
        block = jnp.concatenate([low, block, high], axis=dim)
    return block


def advance(padded):
    center = padded[:, 1:-1, 1:-1]
    east = padded[:, 2:, 1:-1]
    west = padded[:, :-2, 1:-1]
    north = padded[:, 1:-1, 2:]
    south = padded[:, 1:-1, :-2]
    upper = jnp.roll(center, -1, 3)
    lower = jnp.roll(center, 1, 3)
    laplace = east + west + north + south + upper + lower - 6.0 * center
    carried = (
        center[0:1] * (east - west) * 0.5
        + center[1:2] * (north - south) * 0.5
        + center[2:3] * (upper - lower) * 0.5
    )
    return center + time_step * (viscosity * laplace - carried)


def rotations(block, axis):
    return [block] + [shift(block, axis, by) for by in range(1, lax.axis_size(axis))]


def scattered(pieces_of, axis):
    count, own = lax.axis_size(axis), lax.axis_index(axis)
    parts = [pieces_of(own)]
    for by in range(1, count):
        parts.append(shift(pieces_of((own + by) % count), axis, by))
    return parts


BIG = pltpu.CompilerParams(vmem_limit_bytes=48 * 1024 * 1024)
FLOAT = jnp.float32
HALF = jnp.bfloat16


def like(shape, dtype):
    return jax.ShapeDtypeStruct(shape, dtype)


def whole_spec(shape):
    return pl.BlockSpec(shape, lambda *_: (0,) * len(shape))


def turn(block, by, groups):
    rows = block.shape[0] // groups
    cube = block.astype(FLOAT).reshape(groups, rows, block.shape[1])
    return pltpu.roll(cube, by % rows, 1).reshape(block.shape)


def to_patches(field):
    fields, depth, span, length = field.shape
    high, long = span // PATCH, length // PATCH
    flat = PATCH * PATCH
    cells = flat * PATCH

    def kernel(field_ref, out_ref):
        row = lax.broadcasted_iota(jnp.int32, (length, length), 0)
        col = lax.broadcasted_iota(jnp.int32, (length, length), 1)
        pick = (col == (row % long) * PATCH + row // long).astype(HALF)
        row = lax.broadcasted_iota(jnp.int32, (flat, cells), 0)
        col = lax.broadcasted_iota(jnp.int32, (flat, cells), 1)
        inside, deep = row == col // PATCH, col % PATCH
        grids = []
        for part in range(high):
            for index in range(fields):
                brick = field_ref[index, :, part * PATCH : (part + 1) * PATCH, :]
                brick = brick.reshape(flat, length).astype(HALF)
                grids.append(
                    lax.dot_general(
                        pick, brick, (((1,), (1,)), ((), ())), preferred_element_type=FLOAT
                    ).astype(HALF)
                )
        total = jnp.zeros((high * fields * long, cells), FLOAT)
        for step in range(PATCH):
            rows = jnp.concatenate(
                [grid[step * long : (step + 1) * long] for grid in grids], axis=0
            )
            place = (inside & (deep == step)).astype(HALF)
            total = total + jnp.dot(rows, place, preferred_element_type=FLOAT)
        for part in range(high):
            for index in range(fields):
                at = (part * fields + index) * long
                out_ref[
                    part * long : (part + 1) * long, index * cells : (index + 1) * cells
                ] = total[at : at + long].astype(HALF)

    return pl.pallas_call(
        kernel, out_shape=like((high * long, fields * cells), HALF), compiler_params=BIG
    )(field)


def axis_word(axis):
    return lax.axis_index(axis).astype(jnp.int32).reshape(1)


def embed(parts, weight):
    count, rows, cols = len(parts), parts[0].shape[0], weight.shape[1]

    def kernel(own_ref, *refs):
        weight_ref, out_ref = refs[count], refs[count + 1]
        for by in range(count):
            source = lax.rem(own_ref[0] - by + count, count)
            out_ref[pl.ds(pl.multiple_of(source * rows, rows), rows), :] = jnp.dot(
                refs[by][...], weight_ref[...], preferred_element_type=FLOAT
            ).astype(HALF)

    return pl.pallas_call(
        kernel,
        out_shape=like((count * rows, cols), HALF),
        in_specs=[pl.BlockSpec(memory_space=pltpu.SMEM)]
        + [pl.BlockSpec(memory_space=pltpu.VMEM)] * (count + 1),
        compiler_params=BIG,
    )(axis_word("ch"), *parts, weight)


def conv_layer(act, kernels, layer, rows_y, rows_z):
    near = jnp.stack(rotations(act, "ch"))
    below = shift(near, SPLIT, 1)
    above = shift(near, SPLIT, -1)
    count, rows, cols = near.shape
    width = count * cols

    def kernel(own_ref, below_ref, near_ref, above_ref, act_ref, taps_ref, pre_ref, out_ref, planes, total):
        step = pl.program_id(0)

        @pl.when(step == 0)
        def _():
            for plane, source in enumerate((below_ref, near_ref, above_ref)):
                for by in range(count):
                    place = lax.rem(own_ref[0] - by + count, count)
                    at = pl.ds(pl.multiple_of(place * cols, cols), cols)
                    planes[plane, rows_z : rows_z + rows, at] = source[by]
                    planes[plane, :rows_z, at] = source[by, rows - rows_z :]
                    planes[plane, rows_z + rows :, at] = source[by, :rows_z]
            total[...] = jnp.zeros_like(total)

        first = pl.multiple_of(lax.rem(step, 3) * rows_z, rows_z)
        left = planes[step // 3, pl.ds(first, rows), :]
        right = jnp.concatenate([taps_ref[0, index] for index in range(3)], axis=1)
        total[...] += jnp.dot(left, right, preferred_element_type=FLOAT)

        @pl.when(step == 8)
        def _():
            pre = (
                turn(total[:, :cols], 1, rows_y)
                + total[:, cols : 2 * cols]
                + turn(total[:, 2 * cols :], -1, rows_y)
            )
            pre_ref[...] = pre
            out_ref[...] = (act_ref[...].astype(FLOAT) + pre / (1.0 + jnp.exp(-pre))).astype(HALF)

    pre, out = pl.pallas_call(
        kernel,
        grid=(9,),
        out_shape=(like((rows, cols), FLOAT), like((rows, cols), HALF)),
        in_specs=[pl.BlockSpec(memory_space=pltpu.SMEM)]
        + [whole_spec(near.shape)] * 3
        + [
            whole_spec(act.shape),
            pl.BlockSpec((1, 3, width, cols), lambda step: (layer, step, 0, 0)),
        ],
        out_specs=(whole_spec((rows, cols)), whole_spec((rows, cols))),
        scratch_shapes=[
            pltpu.VMEM((3, rows + 2 * rows_z, width), HALF),
            pltpu.VMEM((rows, 3 * cols), FLOAT),
        ],
        compiler_params=BIG,
    )(axis_word("ch"), below, near, above, act, kernels)
    return (pre, out, near)


def give(own_ref, total, cols, count, first_ref, piece_refs):
    for by in range(count):
        place = lax.rem(own_ref[0] + by, count)
        part = total[:, pl.ds(pl.multiple_of(place * cols, cols), cols)]
        if by == 0:
            first_ref[...] = part
        else:
            piece_refs[by - 1][...] = part.astype(HALF)


def conv_back(errors, kernels, layer, rows_y, rows_z, count):
    planes, rows, cols = errors.shape
    width = count * cols

    def kernel(own_ref, *refs):
        error_refs, taps_ref, first_ref = refs[:3], refs[3], refs[4]
        piece_refs, sides, total = refs[5 : 4 + count], refs[4 + count], refs[5 + count]
        step = pl.program_id(0)

        @pl.when(step == 0)
        def _():
            for plane in range(3):
                source = error_refs[plane][0]
                wide = jnp.concatenate(
                    [
                        turn(source, -1, rows_y).astype(HALF),
                        source,
                        turn(source, 1, rows_y).astype(HALF),
                    ],
                    axis=1,
                )
                sides[plane, rows_z : rows_z + rows] = wide
                sides[plane, :rows_z] = wide[rows - rows_z :]
                sides[plane, rows_z + rows :] = wide[:rows_z]
            total[...] = jnp.zeros_like(total)

        first = pl.multiple_of((2 - lax.rem(step, 3)) * rows_z, rows_z)
        left = sides[step // 3, pl.ds(first, rows), :]
        right = jnp.concatenate([taps_ref[0, index] for index in range(3)], axis=1)
        total[...] += lax.dot_general(
            left, right, (((1,), (1,)), ((), ())), preferred_element_type=FLOAT
        )

        @pl.when(step == 8)
        def _():
            give(own_ref, total, cols, count, first_ref, piece_refs)

    def plane_spec(offset):
        return pl.BlockSpec(
            (1, rows, cols), lambda step, word: (lax.rem(word[1] + offset + planes, planes), 0, 0)
        )

    word = jnp.concatenate([axis_word("ch"), axis_word(SPLIT)])
    return pl.pallas_call(
        kernel,
        grid_spec=pltpu.PrefetchScalarGridSpec(
            num_scalar_prefetch=1,
            grid=(9,),
            in_specs=[
                plane_spec(1),
                plane_spec(0),
                plane_spec(-1),
                pl.BlockSpec((1, 3, width, cols), lambda step, word: (layer, step, 0, 0)),
            ],
            out_specs=[whole_spec((rows, cols))] * count,
            scratch_shapes=[
                pltpu.VMEM((3, rows + 2 * rows_z, 3 * cols), HALF),
                pltpu.VMEM((rows, width), FLOAT),
            ],
        ),
        out_shape=[like((rows, cols), FLOAT)] + [like((rows, cols), HALF)] * (count - 1),
        compiler_params=BIG,
    )(word, errors, errors, errors, kernels)


def predict(parts, changes, weight, mask, channels):
    count = len(parts)
    rows, cols = parts[0].shape
    short, block = changes[0].shape
    width = count * cols

    def kernel(own_ref, *refs):
        part_refs, change_refs = refs[:count], refs[count : 2 * count]
        weight_ref, mask_ref = refs[2 * count], refs[2 * count + 1]
        outs = refs[2 * count + 2 :]
        top_ref, error_ref, sums_ref, first_ref = outs[:4]
        piece_refs, held = outs[4 : 3 + count], outs[3 + count]
        for by in range(count):
            place = lax.rem(own_ref[0] - by + count, count)
            top_ref[:, pl.ds(pl.multiple_of(place * cols, cols), cols)] = part_refs[by][...]
            held[pl.ds(pl.multiple_of(place * short, short), short), :] = change_refs[by][...]
        pred = jnp.dot(top_ref[...], weight_ref[...], preferred_element_type=FLOAT)
        resid = held[...].astype(FLOAT) + pred
        mask = mask_ref[...]
        marked = mask * resid
        error = marked.astype(HALF)
        error_ref[...] = error
        sums_ref[0] = jnp.full((8, 128), jnp.sum(marked * resid), FLOAT)
        sums_ref[1] = jnp.full((8, 128), jnp.sum(mask), FLOAT)
        total = refs[-1]
        total[...] = lax.dot_general(
            error, weight_ref[...], (((1,), (1,)), ((), ())), preferred_element_type=FLOAT
        )
        give(own_ref, total, cols, count, first_ref, piece_refs)

    return pl.pallas_call(
        kernel,
        in_specs=[pl.BlockSpec(memory_space=pltpu.SMEM)]
        + [pl.BlockSpec(memory_space=pltpu.VMEM)] * (2 * count + 2),
        out_shape=[
            like((rows, width), HALF),
            like((rows, block), HALF),
            like((2, 8, 128), FLOAT),
            like((rows, cols), FLOAT),
        ]
        + [like((rows, cols), HALF)] * (count - 1),
        scratch_shapes=[pltpu.VMEM((rows, block), HALF), pltpu.VMEM((rows, width), FLOAT)],
        compiler_params=BIG,
    )(axis_word("ch"), *parts, *changes, weight, mask)


def kernel_step(every, errors, scale, kernels, moments, seconds, layer, kept, rows_y, rows_z):
    planes, count, points, lane = every.shape
    cols = errors.shape[2]
    rows = moments.shape[2]
    each = lane // rows
    blocks = -(-9 // each)

    def kernel(word_ref, scale_ref, every_ref, errors_ref, w_ref, m_ref, v_ref, *refs):
        new_w, new_m, new_v, slots, total = refs[-5:]
        offset = lax.rem(word_ref[0] * rows, lane)
        lanes = lax.broadcasted_iota(jnp.int32, (points, lane), 1)

        def prepare(plane, carry):
            own = every_ref[plane, 0].astype(FLOAT)
            for slot in range(each):
                moved = pltpu.roll(own, lax.rem(slot * rows - offset + lane, lane), 1)
                inside = (lanes >= slot * rows) & (lanes < (slot + 1) * rows)
                moved = jnp.where(inside, moved, 0.0).astype(HALF)
                slots[slot, plane, rows_z : rows_z + points] = moved
                slots[slot, plane, :rows_z] = moved[points - rows_z :]
                slots[slot, plane, rows_z + points :] = moved[:rows_z]
            return carry

        lax.fori_loop(0, planes, prepare, 0)
        total[...] = jnp.zeros_like(total)

        def gather(plane, carry):
            left = []
            for block in range(blocks):
                value = None
                for slot in range(each):
                    pair = block * each + slot
                    if pair < 9:
                        source = lax.rem(plane + pair // 3 - 1 + planes, planes)
                        part = slots[slot, source, pl.ds((pair % 3) * rows_z, points), :]
                        value = part if value is None else value + part
                left.append(value)
            left = jnp.concatenate(left, axis=1)
            error = errors_ref[plane]
            right = jnp.concatenate(
                [
                    turn(error, -1, rows_y).astype(HALF),
                    error,
                    turn(error, 1, rows_y).astype(HALF),
                ],
                axis=1,
            )
            total[...] += lax.dot_general(
                left, right, (((0,), (0,)), ((), ())), preferred_element_type=FLOAT
            )
            return carry

        lax.fori_loop(0, planes, gather, 0)
        for tap in range(27):
            at = (tap // 3) * rows
            grad = total[at : at + rows, (tap % 3) * cols : (tap % 3 + 1) * cols] * scale_ref[0]
            weight_next, moment_next, second_next = adam(
                w_ref[0, tap], m_ref[0, tap], v_ref[0, tap], grad
            )
            new_w[tap] = weight_next
            new_m[0, tap] = moment_next
            new_v[0, tap] = second_next

    state_spec = pl.BlockSpec((1, 27, rows, cols), lambda step, word: (layer, 0, 0, 0))
    extra = list(kept)
    place = axis_word(SPLIT)
    word = jnp.concatenate([place, (axis_word("ch") - place * rows // lane + count) % count])
    return pl.pallas_call(
        kernel,
        grid_spec=pltpu.PrefetchScalarGridSpec(
            num_scalar_prefetch=1,
            grid=(1,),
            in_specs=[
                pl.BlockSpec(memory_space=pltpu.SMEM),
                pl.BlockSpec((planes, 1, points, lane), lambda step, word: (0, word[1], 0, 0)),
                whole_spec(errors.shape),
                pl.BlockSpec((1, 27, rows, cols), lambda step, word: (layer, 0, word[0], 0)),
                state_spec,
                state_spec,
            ]
            + [pl.BlockSpec(memory_space=pl.ANY)] * len(extra),
            out_specs=[whole_spec((27, rows, cols)), state_spec, state_spec],
            scratch_shapes=[
                pltpu.VMEM((each, planes, points + 2 * rows_z, lane), HALF),
                pltpu.VMEM((blocks * lane, 3 * cols), FLOAT),
            ],
        ),
        out_shape=[
            like((27, rows, cols), HALF),
            like(moments.shape, FLOAT),
            like(seconds.shape, FLOAT),
        ],
        input_output_aliases={7: 1, 8: 2} if extra else {},
        compiler_params=BIG,
    )(word, scale.reshape(1), every, errors, kernels, moments, seconds, *extra)


def settle(gathered, shape, layer, kept):
    count, taps, rows, cols = gathered.shape

    def kernel(*refs):
        refs[-1][0] = refs[0][0]

    extra = list(kept)
    return pl.pallas_call(
        kernel,
        grid=(count,),
        in_specs=[pl.BlockSpec((1, taps, rows, cols), lambda step: (step, 0, 0, 0))]
        + [pl.BlockSpec(memory_space=pl.ANY)] * len(extra),
        out_specs=pl.BlockSpec((1, taps, rows, cols), lambda step: (layer, 0, step, 0)),
        out_shape=like(shape, HALF),
        input_output_aliases={1: 0} if extra else {},
        compiler_params=BIG,
    )(gathered, *extra)


def silu_slope(value):
    sig = jax.nn.sigmoid(value)
    return sig * (1.0 + value * (1.0 - sig))


def adam(weight, moment, second, grad):
    moment_next = beta_one * moment + (1.0 - beta_one) * grad
    second_next = beta_two * second + (1.0 - beta_two) * grad * grad
    weight_next = weight.astype(jnp.float32) - learn_rate * (moment_next / bias_one) / (
        jnp.sqrt(second_next / bias_two) + adam_eps
    )
    return (weight_next.astype(jnp.bfloat16), moment_next, second_next)


def total_of(block, axis):
    by = 1
    while by < lax.axis_size(axis):
        block = block + shift(block, axis, by)
        by *= 2
    return block


def body(flow, embed_w, conv_w, dec_w, conv_m, conv_v, dec_m, dec_v, loss_mask):
    rows_y = flow.shape[2] * lax.axis_size("ch") // PATCH
    rows_z = flow.shape[3] // PATCH
    width = conv_w.shape[2]
    channels = conv_w.shape[3]
    block = dec_w.shape[1]
    place = lax.axis_index(SPLIT)
    dec_rows = dec_m.shape[0]

    rounded = flow.astype(HALF).astype(FLOAT)
    patches = to_patches(flow)
    every_patch = lax.all_gather(patches, "ch", axis=0)
    count = lax.axis_size("ch")
    embedded = jnp.dot(
        every_patch.reshape(-1, patches.shape[1]), embed_w, preferred_element_type=FLOAT
    ).astype(HALF)

    state = with_halo(flow, ((SPLIT, 1), ("ch", 2)), FLOW_STEPS)
    for step in range(FLOW_STEPS):
        state = advance(state)
    change = to_patches(rounded - state)
    changes = scattered(
        lambda k: lax.dynamic_slice_in_dim(change, k * block, block, 1), "ch"
    )

    pre_one, act_one, near_one = conv_layer(embedded, conv_w, 0, rows_y, rows_z)
    pre_two, act_two, near_two = conv_layer(act_one, conv_w, 1, rows_y, rows_z)

    mask = loss_mask.reshape(-1, 1).astype(FLOAT)
    top, d_pred, sums, d_act_two, *pieces = predict(
        rotations(act_two, "ch"), changes, dec_w, mask, channels
    )
    sums = total_of(total_of(sums, "ch"), SPLIT)[:, 0, 0]
    denom = jnp.maximum(sums[1] / count, 1.0) * OUT
    loss = sums[0] / denom
    scale = 2.0 / denom

    def reduced(own, pieces):
        for by, piece in enumerate(pieces):
            own = own + shift(piece, "ch", by + 1).astype(FLOAT)
        return own

    d_act_two = reduced(d_act_two, pieces)
    d_pre_two = (d_act_two * silu_slope(pre_two)).astype(HALF)
    errors_two = lax.all_gather(d_pre_two, SPLIT, axis=0)
    own_back, *pieces = conv_back(errors_two, conv_w, 1, rows_y, rows_z, count)
    d_act_one = d_act_two + reduced(own_back, pieces)
    d_pre_one = (d_act_one * silu_slope(pre_one)).astype(HALF)
    errors_one = lax.all_gather(d_pre_one, SPLIT, axis=0)

    grad_dec = lax.dot_general(top, d_pred, (((0,), (0,)), ((), ())), preferred_element_type=FLOAT)
    grad_dec = lax.all_to_all(
        grad_dec.astype(HALF).reshape(-1, dec_rows, block), SPLIT, 0, 0, tiled=False
    )
    grad_dec = jnp.sum(grad_dec.astype(FLOAT), axis=0) * scale
    dec_own = lax.dynamic_slice_in_dim(dec_w, place * dec_rows, dec_rows, 0)
    dec_shard, dec_m_next, dec_v_next = adam(dec_own, dec_m, dec_v, grad_dec)
    dec_next = lax.all_gather(dec_shard, SPLIT, axis=0, tiled=True)

    rows_two = lax.all_gather(near_two, SPLIT, axis=0)
    rows_one = lax.all_gather(near_one, SPLIT, axis=0)
    two_shard, *moments = kernel_step(
        rows_two, errors_two, scale, conv_w, conv_m, conv_v, 1, (), rows_y, rows_z
    )
    one_shard, *moments = kernel_step(
        rows_one, errors_one, scale, conv_w, conv_m, conv_v, 0, moments, rows_y, rows_z
    )
    conv_next = settle(lax.all_gather(two_shard, SPLIT, axis=0), conv_w.shape, 1, ())
    conv_next = settle(lax.all_gather(one_shard, SPLIT, axis=0), conv_w.shape, 0, (conv_next,))
    return (
        state,
        loss,
        conv_next,
        dec_next,
        *moments,
        dec_m_next,
        dec_v_next,
    )


def solution(mesh):
    return jax.shard_map(
        body,
        mesh=mesh,
        in_specs=(
            P(None, ("grp", "sp"), "ch", None),
            P(None, "ch"),
            P(None, None, None, "ch"),
            P(None, "ch"),
            P(None, None, ("grp", "sp"), "ch"),
            P(None, None, ("grp", "sp"), "ch"),
            P(("grp", "sp"), "ch"),
            P(("grp", "sp"), "ch"),
            P(("grp", "sp"), None, None),
        ),
        out_specs=(
            P(None, ("grp", "sp"), "ch", None),
            P(),
            P(None, None, None, "ch"),
            P(None, "ch"),
            P(None, None, ("grp", "sp"), "ch"),
            P(None, None, ("grp", "sp"), "ch"),
            P(("grp", "sp"), "ch"),
            P(("grp", "sp"), "ch"),
        ),
        check_vma=False,
    )
```

```python
import jax
import jax.numpy as jnp
from jax import lax
from jax.experimental import pallas as pl
from jax.experimental.pallas import tpu as pltpu
from jax.sharding import PartitionSpec as P

PATCH = 8
FLOW_STEPS = 2
OUT = 2048
SPLIT = ("grp", "sp")


time_step = 0.1
viscosity = 0.2
beta_one = 0.9
beta_two = 0.95
learn_rate = 0.001
adam_eps = 1e-08
bias_one = 0.9999734386011124
bias_two = 0.994079470779666


def shift(block, axis, by):
    count = lax.axis_size(axis)
    return lax.ppermute(block, axis, [(i, (i + by) % count) for i in range(count)])


def with_halo(block, sides, width, hold):
    for axis, dim in sides:
        low = lax.slice_in_dim(block, block.shape[dim] - width, None, axis=dim)
        high = lax.slice_in_dim(block, 0, width, axis=dim)
        low, high, hold = lax.optimization_barrier((low, high, hold))
        low, high = shift(low, axis, 1), shift(high, axis, -1)
        block = jnp.concatenate([low, block, high], axis=dim)
    return block


def advance(padded):
    center = padded[:, 1:-1, 1:-1]
    east = padded[:, 2:, 1:-1]
    west = padded[:, :-2, 1:-1]
    north = padded[:, 1:-1, 2:]
    south = padded[:, 1:-1, :-2]
    upper = jnp.roll(center, -1, 3)
    lower = jnp.roll(center, 1, 3)
    laplace = east + west + north + south + upper + lower - 6.0 * center
    carried = (
        center[0:1] * (east - west) * 0.5
        + center[1:2] * (north - south) * 0.5
        + center[2:3] * (upper - lower) * 0.5
    )
    return center + time_step * (viscosity * laplace - carried)


def rotations(block, axis):
    return [block] + [shift(block, axis, by) for by in range(1, lax.axis_size(axis))]


def scattered(pieces_of, axis):
    count, own = lax.axis_size(axis), lax.axis_index(axis)
    parts = [pieces_of(own)]
    for by in range(1, count):
        parts.append(shift(pieces_of((own + by) % count), axis, by))
    return parts


BIG = pltpu.CompilerParams(vmem_limit_bytes=48 * 1024 * 1024)
FULL = pltpu.CompilerParams(vmem_limit_bytes=60 * 1024 * 1024)
FLOAT = jnp.float32
HALF = jnp.bfloat16


def like(shape, dtype):
    return jax.ShapeDtypeStruct(shape, dtype)


def whole_spec(shape):
    return pl.BlockSpec(shape, lambda *_: (0,) * len(shape))


def turn(block, by, groups):
    rows = block.shape[0] // groups
    cube = block.astype(FLOAT).reshape(groups, rows, block.shape[1])
    return pltpu.roll(cube, by % rows, 1).reshape(block.shape)


def to_patches(field):
    fields, depth, span, length = field.shape
    high, long = span // PATCH, length // PATCH
    flat = PATCH * PATCH
    cells = flat * PATCH

    def kernel(field_ref, out_ref):
        row = lax.broadcasted_iota(jnp.int32, (length, length), 0)
        col = lax.broadcasted_iota(jnp.int32, (length, length), 1)
        pick = (col == (row % long) * PATCH + row // long).astype(HALF)
        row = lax.broadcasted_iota(jnp.int32, (flat, cells), 0)
        col = lax.broadcasted_iota(jnp.int32, (flat, cells), 1)
        inside, deep = row == col // PATCH, col % PATCH
        grids = []
        for part in range(high):
            for index in range(fields):
                brick = field_ref[index, :, part * PATCH : (part + 1) * PATCH, :]
                brick = brick.reshape(flat, length).astype(HALF)
                grids.append(
                    lax.dot_general(
                        pick, brick, (((1,), (1,)), ((), ())), preferred_element_type=FLOAT
                    ).astype(HALF)
                )
        total = jnp.zeros((high * fields * long, cells), FLOAT)
        for step in range(PATCH):
            rows = jnp.concatenate(
                [grid[step * long : (step + 1) * long] for grid in grids], axis=0
            )
            place = (inside & (deep == step)).astype(HALF)
            total = total + jnp.dot(rows, place, preferred_element_type=FLOAT)
        for part in range(high):
            for index in range(fields):
                at = (part * fields + index) * long
                out_ref[
                    part * long : (part + 1) * long, index * cells : (index + 1) * cells
                ] = total[at : at + long].astype(HALF)

    return pl.pallas_call(
        kernel, out_shape=like((high * long, fields * cells), HALF), compiler_params=BIG
    )(field)


def axis_word(axis):
    return lax.axis_index(axis).astype(jnp.int32).reshape(1)


def after(value, *others):
    return lax.optimization_barrier((value, others))[0]


def ring_pieces(block, axis):
    count, rows = lax.axis_size(axis), block.shape[0]
    pieces, up, down = [(0, 0, block)], block, block
    for by in range(1, (count + 1) // 2):
        up, down = shift(up, axis, 1), shift(down, axis, -1)
        pieces += [(by, 0, up), (count - by, 0, down)]
    if count % 2 == 0:
        half = rows // 2
        pieces.append((count // 2, 0, shift(up[:half], axis, 1)))
        pieces.append((count // 2, half, shift(down[half:], axis, -1)))
    return pieces


def embed(pieces, rows, weight):
    count, cols = lax.axis_size("ch"), weight.shape[1]
    marks = [(by, first, piece.shape[0]) for by, first, piece in pieces]

    def kernel(own_ref, *refs):
        weight_ref, out_ref = refs[-2:]
        for (by, first, long), piece_ref in zip(marks, refs):
            at = lax.rem(own_ref[0] - by + count, count) * rows + first
            out_ref[pl.ds(pl.multiple_of(at, long), long), :] = jnp.dot(
                piece_ref[...], weight_ref[...], preferred_element_type=FLOAT
            ).astype(HALF)

    arrays = [piece for _, _, piece in pieces] + [weight]
    return pl.pallas_call(
        kernel,
        grid=(1,),
        out_shape=like((count * rows, cols), HALF),
        in_specs=[pl.BlockSpec(memory_space=pltpu.SMEM)] + [whole_spec(a.shape) for a in arrays],
        out_specs=whole_spec((count * rows, cols)),
        compiler_params=BIG,
    )(axis_word("ch"), *arrays)


def fetch(taps_ref, layer, held, sems, pairs):
    copies = {}
    for slot, pair in enumerate(pairs):
        copies[pair] = pltpu.make_async_copy(
            taps_ref.at[layer, pl.ds(3 * pair, 3)], held.at[slot], sems.at[slot]
        )
        copies[pair].start()
    return copies


def conv_planes(sources, kernels, layer, rows_y, rows_z, planes, tail):
    count, rows, cols = sources[0].shape
    width = count * cols
    pairs = [3 * plane + down for plane in planes for down in range(3)]

    def kernel(own_ref, *refs):
        source_refs, taps_ref = refs[: len(planes)], refs[len(planes)]
        grids, held, sems = refs[-3:]
        copies = fetch(taps_ref, layer, held, sems, pairs)
        for plane, source in enumerate(source_refs):
            for by in range(count):
                place = lax.rem(own_ref[0] - by + count, count)
                at = pl.ds(pl.multiple_of(place * cols, cols), cols)
                grids[plane, rows_z : rows_z + rows, at] = source[by]
                grids[plane, :rows_z, at] = source[by, rows - rows_z :]
                grids[plane, rows_z + rows :, at] = source[by, :rows_z]
        total = None
        for slot, pair in enumerate(pairs):
            copies[pair].wait()
            left = grids[slot // 3, pl.ds((slot % 3) * rows_z, rows), :]
            right = jnp.concatenate([held[slot, index] for index in range(3)], axis=1)
            part = jnp.dot(left, right, preferred_element_type=FLOAT)
            total = part if total is None else total + part
        if not tail:
            refs[-4][...] = total
            return
        act_ref, other_ref, pre_ref, out_ref = refs[len(planes) + 1 : len(planes) + 5]
        total = total + other_ref[...]
        pre = (
            turn(total[:, :cols], 1, rows_y)
            + total[:, cols : 2 * cols]
            + turn(total[:, 2 * cols :], -1, rows_y)
        )
        pre_ref[...] = pre
        out_ref[...] = (act_ref[...].astype(FLOAT) + pre / (1.0 + jnp.exp(-pre))).astype(HALF)

    outs = [like((rows, 3 * cols), FLOAT)]
    if tail:
        outs = [like((rows, cols), FLOAT), like((rows, cols), HALF)]
    return pl.pallas_call(
        kernel,
        grid=(1,),
        out_shape=outs,
        in_specs=[pl.BlockSpec(memory_space=pltpu.SMEM)]
        + [whole_spec(source.shape) for source in sources]
        + [pl.BlockSpec(memory_space=pl.ANY)]
        + [whole_spec(array.shape) for array in tail],
        out_specs=[whole_spec(out.shape) for out in outs],
        scratch_shapes=[
            pltpu.VMEM((len(planes), rows + 2 * rows_z, width), HALF),
            pltpu.VMEM((len(pairs), 3, width, cols), HALF),
            pltpu.SemaphoreType.DMA((len(pairs),)),
        ],
        compiler_params=BIG,
    )(axis_word("ch"), *sources, kernels, *tail)


def conv_layer(act, kernels, layer, rows_y, rows_z, hold):
    near = jnp.stack(rotations(act, "ch"))
    below, above = shift(near, SPLIT, 1), shift(near, SPLIT, -1)
    (middle,) = conv_planes((near,), kernels, layer, rows_y, rows_z, (1,), ())
    below = after(below, middle, *hold)
    pre, out = conv_planes(
        (below, above), kernels, layer, rows_y, rows_z, (0, 2), (act, middle)
    )
    return (pre, out, near)


def split_up(value):
    high = value.astype(HALF)
    rest = value - high.astype(FLOAT)
    middle = rest.astype(HALF)
    return [high, middle, (rest - middle.astype(FLOAT)).astype(HALF)]


def give(own_ref, total, cols, count, first_ref, piece_refs):
    for by in range(count):
        place = lax.rem(own_ref[0] + by, count)
        part = total[:, pl.ds(pl.multiple_of(place * cols, cols), cols)]
        if by == 0:
            first_ref[...] = part
        else:
            piece_refs[by - 1][: part.shape[0]] = part.astype(HALF)


def conv_back(errors, kernels, layer, rows_y, rows_z, count):
    planes, _, cols = errors.shape
    rows, width = rows_y * rows_z, count * cols
    pairs = list(range(9))

    def kernel(own_ref, *refs):
        error_refs, taps_ref, first_ref = refs[:3], refs[3], refs[4]
        piece_refs, sides, held, sems, total = refs[5 : 4 + count], *refs[4 + count :]
        copies = fetch(taps_ref, layer, held, sems, pairs)
        for plane in range(3):
            source = error_refs[plane][0]
            wide = jnp.concatenate(
                [
                    turn(source, -1, rows_y).astype(HALF),
                    source,
                    turn(source, 1, rows_y).astype(HALF),
                ],
                axis=1,
            )
            sides[plane, rows_z : rows_z + rows] = wide
            sides[plane, :rows_z] = wide[rows - rows_z :]
            sides[plane, rows_z + rows :] = wide[:rows_z]
        value = None
        for pair in pairs:
            copies[pair].wait()
            left = sides[pair // 3, pl.ds((2 - pair % 3) * rows_z, rows), :]
            right = jnp.concatenate([held[pair, index] for index in range(3)], axis=1)
            part = lax.dot_general(
                left, right, (((1,), (1,)), ((), ())), preferred_element_type=FLOAT
            )
            value = part if value is None else value + part
        total[...] = value
        give(own_ref, total, cols, count, first_ref, piece_refs)

    def plane_spec(offset):
        return pl.BlockSpec(
            (1, rows, cols), lambda step, word: (lax.rem(word[1] + offset + planes, planes), 0, 0)
        )

    word = jnp.concatenate([axis_word("ch"), axis_word(SPLIT)])
    return pl.pallas_call(
        kernel,
        grid_spec=pltpu.PrefetchScalarGridSpec(
            num_scalar_prefetch=1,
            grid=(1,),
            in_specs=[
                plane_spec(1),
                plane_spec(0),
                plane_spec(-1),
                pl.BlockSpec(memory_space=pl.ANY),
            ],
            out_specs=[whole_spec((rows, cols))] * count,
            scratch_shapes=[
                pltpu.VMEM((3, rows + 2 * rows_z, 3 * cols), HALF),
                pltpu.VMEM((9, 3, width, cols), HALF),
                pltpu.SemaphoreType.DMA((9,)),
                pltpu.VMEM((rows, width), FLOAT),
            ],
        ),
        out_shape=[like((rows, cols), FLOAT)] + [like((rows, cols), HALF)] * (count - 1),
        compiler_params=BIG,
    )(word, errors, errors, errors, kernels)


def step_back(own, pieces, pre, extra):
    rows, cols = own.shape
    stats = extra.shape[0] != rows

    def kernel(own_ref, *refs):
        piece_refs, pre_ref, extra_ref = refs[: len(pieces)], refs[-4], refs[-3]
        error_ref, send_ref = refs[-2:]
        error = own_ref[...]
        for ref in piece_refs:
            error = error + ref[:rows].astype(FLOAT)
        if not stats:
            error = error + extra_ref[...]
        error_ref[...] = error
        send_ref[:rows] = (error * silu_slope(pre_ref[...])).astype(HALF)
        if stats:
            squares = extra_ref[:1]
            for ref in piece_refs:
                for term in range(3):
                    squares = squares + ref[rows + term : rows + term + 1].astype(FLOAT)
            marked = extra_ref[1:2]
            coarse = jnp.floor(marked / 128.0)
            terms = split_up(squares) + [coarse.astype(HALF), (marked - 128.0 * coarse).astype(HALF)]
            terms.append(jnp.zeros((11, cols), HALF))
            send_ref[rows:] = jnp.concatenate([term.astype(FLOAT) for term in terms]).astype(HALF)

    arrays = [own, *pieces, pre, extra]
    outs = [like((rows, cols), FLOAT), like((rows + 16 * stats, cols), HALF)]
    return pl.pallas_call(
        kernel,
        grid=(1,),
        in_specs=[whole_spec(array.shape) for array in arrays],
        out_specs=[whole_spec(out.shape) for out in outs],
        out_shape=outs,
        compiler_params=BIG,
    )(*arrays)


def predict(parts, changes, weight, mask, channels):
    count = len(parts)
    rows, cols = parts[0].shape
    short, block = changes[0].shape
    width = count * cols

    def kernel(own_ref, *refs):
        part_refs, change_refs = refs[:count], refs[count : 2 * count]
        weight_ref, mask_ref = refs[2 * count], refs[2 * count + 1]
        outs = refs[2 * count + 2 :]
        top_ref, error_ref, sums_ref, first_ref = outs[:4]
        piece_refs, held = outs[4 : 3 + count], outs[3 + count]
        for by in range(count):
            place = lax.rem(own_ref[0] - by + count, count)
            top_ref[:, pl.ds(pl.multiple_of(place * cols, cols), cols)] = part_refs[by][...]
            held[pl.ds(pl.multiple_of(place * short, short), short), :] = change_refs[by][...]
        pred = jnp.dot(top_ref[...], weight_ref[...], preferred_element_type=FLOAT)
        resid = held[...].astype(FLOAT) + pred
        mask = mask_ref[...]
        marked = mask * resid
        error = marked.astype(HALF)
        error_ref[...] = error
        squares = jnp.full((1, cols), jnp.sum(marked * resid), FLOAT)
        marks = jnp.full((1, cols), jnp.sum(mask), FLOAT)
        sums_ref[...] = jnp.concatenate([squares, marks, jnp.zeros((6, cols), FLOAT)])
        terms = [term.astype(FLOAT) for term in split_up(squares)]
        terms = jnp.concatenate(terms + [jnp.zeros((13, cols), FLOAT)]).astype(HALF)
        for piece_ref in piece_refs:
            piece_ref[rows:] = terms
        total = refs[-1]
        total[...] = lax.dot_general(
            error, weight_ref[...], (((1,), (1,)), ((), ())), preferred_element_type=FLOAT
        )
        give(own_ref, total, cols, count, first_ref, piece_refs)

    arrays = [*parts, *changes, weight, mask]
    outs = [
        like((rows, width), HALF),
        like((rows, block), HALF),
        like((8, cols), FLOAT),
        like((rows, cols), FLOAT),
    ] + [like((rows + 16, cols), HALF)] * (count - 1)
    return pl.pallas_call(
        kernel,
        grid=(1,),
        in_specs=[pl.BlockSpec(memory_space=pltpu.SMEM)] + [whole_spec(a.shape) for a in arrays],
        out_specs=[whole_spec(out.shape) for out in outs],
        out_shape=outs,
        scratch_shapes=[pltpu.VMEM((rows, block), HALF), pltpu.VMEM((rows, width), FLOAT)],
        compiler_params=BIG,
    )(axis_word("ch"), *arrays)


def spread_slots(every, rows, rows_y, rows_z):
    planes, count, points, lane = every.shape
    each = lane // rows

    def kernel(word_ref, every_ref, slots, held, sem):
        read = pltpu.make_async_copy(every_ref.at[:, word_ref[1]], held, sem)
        read.start()
        offset = lax.rem(word_ref[0] * rows, lane)
        lanes = lax.broadcasted_iota(jnp.int32, (points, lane), 1)
        read.wait()

        def prepare(plane, carry):
            own = held[plane].astype(FLOAT)
            for slot in range(each):
                moved = pltpu.roll(own, lax.rem(slot * rows - offset + lane, lane), 1)
                inside = (lanes >= slot * rows) & (lanes < (slot + 1) * rows)
                moved = jnp.where(inside, moved, 0.0).astype(HALF)
                slots[slot, plane, rows_z : rows_z + points] = moved
                slots[slot, plane, :rows_z] = moved[points - rows_z :]
                slots[slot, plane, rows_z + points :] = moved[:rows_z]
            return carry

        lax.fori_loop(0, planes, prepare, 0)

    shape = (each, planes, points + 2 * rows_z, lane)
    place = axis_word(SPLIT)
    word = jnp.concatenate([place, (axis_word("ch") - place * rows // lane + count) % count])
    return pl.pallas_call(
        kernel,
        grid=(1,),
        in_specs=[pl.BlockSpec(memory_space=pltpu.SMEM), pl.BlockSpec(memory_space=pltpu.HBM)],
        out_specs=whole_spec(shape),
        out_shape=like(shape, HALF),
        scratch_shapes=[pltpu.VMEM((planes, points, lane), HALF), pltpu.SemaphoreType.DMA],
        compiler_params=FULL,
    )(word, every)


def kernel_step(slots, errors, counted, states, layer, kept, dec, rows_y, rows_z):
    each, planes, _, lane = slots.shape
    points, cols = rows_y * rows_z, errors.shape[2]
    rows = states[1].shape[2]
    blocks = -(-9 // each)
    solo = 2 * bool(dec)
    more = dec[1].shape[1] // cols if dec else 0
    chunk = 9

    def kernel(word_ref, slots_ref, errors_ref, counted_ref, w_hbm, m_hbm, v_hbm, *refs):
        dec_refs = refs[: len(dec)]
        refs = refs[len(dec) + len(kept) :]
        new_w, m_out, v_out, loss_ref, *dec_outs = refs[: 4 + solo]
        w_ref, m_ref, v_ref, new_m, new_v, total, sems, out_sems = refs[4 + solo :]
        reads = [
            pltpu.make_async_copy(
                w_hbm.at[layer, :, pl.ds(pl.multiple_of(word_ref[0] * rows, rows), rows)],
                w_ref,
                sems.at[0],
            ),
            pltpu.make_async_copy(m_hbm.at[layer], m_ref, sems.at[1]),
            pltpu.make_async_copy(v_hbm.at[layer], v_ref, sems.at[2]),
        ]
        for read in reads:
            read.start()
        total[...] = jnp.zeros_like(total)

        def gather(plane, carry):
            left = []
            for block in range(blocks):
                value = None
                for slot in range(each):
                    pair = block * each + slot
                    if pair < 9:
                        source = lax.rem(plane + pair // 3 - 1 + planes, planes)
                        part = slots_ref[slot, source, pl.ds((pair % 3) * rows_z, points), :]
                        value = part if value is None else value + part
                left.append(value)
            left = jnp.concatenate(left, axis=1)
            error = errors_ref[plane, :points]
            right = jnp.concatenate(
                [
                    turn(error, -1, rows_y).astype(HALF),
                    error,
                    turn(error, 1, rows_y).astype(HALF),
                ],
                axis=1,
            )
            total[...] += lax.dot_general(
                left, right, (((0,), (0,)), ((), ())), preferred_element_type=FLOAT
            )
            return carry

        lax.fori_loop(0, planes, gather, 0)
        stats = jnp.sum(counted_ref[...].astype(FLOAT), axis=0)
        denom = jnp.maximum(128.0 * stats[3:4, :1] + stats[4:5, :1], 1.0) * OUT
        scale = 2.0 / denom
        squares = (stats[0:1, :1] + stats[1:2, :1]) + stats[2:3, :1]
        loss_ref[...] = jnp.broadcast_to(squares / denom, (8, 128))
        for read in reads:
            read.wait()
        writes = []
        for tap in range(27):
            at = (tap // 3) * rows
            grad = total[at : at + rows, (tap % 3) * cols : (tap % 3 + 1) * cols] * scale
            weight_next, moment_next, second_next = adam(w_ref[tap], m_ref[tap], v_ref[tap], grad)
            new_w[tap] = weight_next
            new_m[tap] = moment_next
            new_v[tap] = second_next
            if tap % chunk == chunk - 1:
                part = pl.ds(tap + 1 - chunk, chunk)
                for source, out, side in ((new_m, m_out, 0), (new_v, v_out, 1)):
                    writes.append(
                        pltpu.make_async_copy(
                            source.at[part],
                            out.at[layer, part],
                            out_sems.at[2 * (tap // chunk) + side],
                        )
                    )
                    writes[-1].start()
        if dec:
            grad_ref, dec_w_ref, dec_m_ref, dec_v_ref = dec_refs
            weight_next, moment_next, second_next = adam(
                dec_w_ref[...], dec_m_ref[...], dec_v_ref[...], grad_ref[...] * scale
            )
            dec_outs[0][...] = moment_next
            dec_outs[1][...] = second_next
            for index in range(more):
                new_w[27 + index] = weight_next[:, index * cols : (index + 1) * cols]
        for write in writes:
            write.wait()

    any_spec = pl.BlockSpec(memory_space=pl.ANY)
    hbm_spec = pl.BlockSpec(memory_space=pltpu.HBM)
    dec_specs = []
    if dec:
        flat = whole_spec(dec[2].shape)
        dec_specs = [flat, pl.BlockSpec(dec[2].shape, lambda step, word: (word[0], 0)), flat, flat]
    outs = [
        like((27 + more, rows, cols), HALF),
        like(states[1].shape, FLOAT),
        like(states[2].shape, FLOAT),
        like((8, 128), FLOAT),
    ] + [like(array.shape, FLOAT) for array in dec[2:]]
    first = 7 + len(dec)
    return pl.pallas_call(
        kernel,
        grid_spec=pltpu.PrefetchScalarGridSpec(
            num_scalar_prefetch=1,
            grid=(1,),
            in_specs=[
                whole_spec(slots.shape),
                whole_spec(errors.shape),
                pl.BlockSpec((planes, 16, cols), lambda step, word: (0, points // 16, 0)),
                hbm_spec,
                hbm_spec,
                hbm_spec,
            ]
            + dec_specs
            + [any_spec] * len(kept),
            out_specs=[
                whole_spec((27 + more, rows, cols)),
                any_spec,
                any_spec,
                whole_spec((8, 128)),
            ]
            + [whole_spec(array.shape) for array in dec[2:]],
            scratch_shapes=[
                pltpu.VMEM((27, rows, cols), HALF),
                pltpu.VMEM((27, rows, cols), FLOAT),
                pltpu.VMEM((27, rows, cols), FLOAT),
                pltpu.VMEM((27, rows, cols), FLOAT),
                pltpu.VMEM((27, rows, cols), FLOAT),
                pltpu.VMEM((blocks * lane, 3 * cols), FLOAT),
                pltpu.SemaphoreType.DMA((3,)),
                pltpu.SemaphoreType.DMA((2 * 27 // chunk,)),
            ],
        ),
        out_shape=outs,
        input_output_aliases={first: 1, first + 1: 2} if kept else {},
        compiler_params=BIG,
    )(axis_word(SPLIT), slots, errors, counted, *states, *dec, *kept)


def settle(gathered, shape, layer):
    count, taps, rows, cols = gathered.shape

    def kernel(from_ref, out_ref):
        out_ref[0] = from_ref[0]

    return pl.pallas_call(
        kernel,
        grid=(count,),
        in_specs=[pl.BlockSpec((1, taps, rows, cols), lambda step: (step, 0, 0, 0))],
        out_specs=pl.BlockSpec((1, taps, rows, cols), lambda step: (layer, 0, step, 0)),
        out_shape=like(shape, HALF),
        compiler_params=BIG,
    )(gathered)


def cross(block, mask):
    count = lax.axis_size(SPLIT)
    return lax.ppermute(block, SPLIT, [(i, i ^ mask) for i in range(count)])


def with_partner(pieces):
    return pieces + [(mask + 1, first, cross(piece, 1)) for mask, first, piece in pieces]


def cube_pieces(block, hold):
    count, long = lax.axis_size(SPLIT), block.shape[0]
    outer = [1 << bit for bit in range(1, (count - 1).bit_length())]
    pieces, last = [(0, 0, block)], []
    if len(outer) == 2:
        one, two = outer
        half = long // 2
        by_one, by_two = cross(block, one), cross(block, two)
        by_one, by_two, _ = lax.optimization_barrier((by_one, by_two, hold))
        pieces += [(one, 0, by_one), (two, 0, by_two)]
        last.append((one + two, 0, cross(by_two[:half], one)))
        last.append((one + two, half, cross(by_one[half:], two)))
    else:
        for bit in outer:
            pieces += [(mask + bit, first, cross(piece, bit)) for mask, first, piece in pieces]
    return pieces, last


def settle_pieces(pieces, layer, kept, dec_shape, dec_kept):
    marks = [(mask, first, piece.shape[0]) for mask, first, piece in pieces]
    count, taps = len(pieces), kept.shape[1]
    _, rows, cols = pieces[0][2].shape
    every = sum(1 + max(0, first + long - taps) for _, first, long in marks)

    def kernel(place_ref, *refs):
        out_ref, dec_ref, sems = refs[-3:]
        copies = []

        def copy(source, target):
            copies.append(pltpu.make_async_copy(source, target, sems.at[len(copies)]))
            copies[-1].start()

        for ref, (mask, first, long) in zip(refs, marks):
            at = pl.ds(pl.multiple_of((place_ref[0] ^ mask) * rows, rows), rows)
            own = min(long, taps - first)
            copy(ref.at[pl.ds(0, own)], out_ref.at[layer, pl.ds(first, own), at])
            for index in range(own, long):
                column = (first + index - taps) * cols
                copy(ref.at[index], dec_ref.at[at, pl.ds(column, cols)])
        for started in copies:
            started.wait()

    any_spec = pl.BlockSpec(memory_space=pl.ANY)
    return pl.pallas_call(
        kernel,
        grid=(1,),
        in_specs=[pl.BlockSpec(memory_space=pltpu.SMEM)]
        + [whole_spec(piece.shape) for _, _, piece in pieces]
        + [any_spec] * (1 + len(dec_kept)),
        out_specs=[any_spec, any_spec],
        out_shape=[like(kept.shape, HALF), like(dec_shape, HALF)],
        scratch_shapes=[pltpu.SemaphoreType.DMA((every,))],
        input_output_aliases={count + 1 + index: index for index in range(1 + len(dec_kept))},
        compiler_params=BIG,
    )(axis_word(SPLIT), *[piece for _, _, piece in pieces], kept, *dec_kept)


def halves(block, bit):
    pairs = block.reshape(block.shape[0] // 2, 2, *block.shape[1:])
    mine = (lax.axis_index(SPLIT) // bit) % 2
    keep = lax.dynamic_index_in_dim(pairs, mine, 1, keepdims=False)
    send = lax.dynamic_index_in_dim(pairs, 1 - mine, 1, keepdims=False)
    return keep, send.astype(HALF)


def halved(keep, send, holds):
    bit, turn_at = 1, 0
    while True:
        sent = after(cross(send, bit), holds[min(turn_at, len(holds) - 1)])
        block = keep.astype(FLOAT) + sent.astype(FLOAT)
        bit, turn_at = 2 * bit, turn_at + 1
        if bit == lax.axis_size(SPLIT):
            return block[0]
        keep, send = halves(block, bit)


def silu_slope(value):
    sig = jax.nn.sigmoid(value)
    return sig * (1.0 + value * (1.0 - sig))


def adam(weight, moment, second, grad):
    moment_next = beta_one * moment + (1.0 - beta_one) * grad
    second_next = beta_two * second + (1.0 - beta_two) * grad * grad
    weight_next = weight.astype(jnp.float32) - learn_rate * (moment_next / bias_one) / (
        jnp.sqrt(second_next / bias_two) + adam_eps
    )
    return (weight_next.astype(jnp.bfloat16), moment_next, second_next)


def body(flow, embed_w, conv_w, dec_w, conv_m, conv_v, dec_m, dec_v, loss_mask):
    rows_y = flow.shape[2] * lax.axis_size("ch") // PATCH
    rows_z = flow.shape[3] // PATCH
    width = conv_w.shape[2]
    channels = conv_w.shape[3]
    block = dec_w.shape[1]
    dec_rows = dec_m.shape[0]
    conv_rows = conv_m.shape[2]

    count = lax.axis_size("ch")
    patches = to_patches(flow)
    pieces = ring_pieces(patches, "ch")
    padded = with_halo(flow, ((SPLIT, 1), ("ch", 2)), FLOW_STEPS, patches)
    by, first, piece = pieces[-1]
    pieces[-1] = (by, first, after(piece, padded))
    embedded = embed(pieces, patches.shape[0], embed_w)

    state = padded
    for step in range(FLOW_STEPS):
        state = advance(state)
    change = to_patches(flow.astype(HALF).astype(FLOAT) - state)
    pre_one, act_one, near_one = conv_layer(embedded, conv_w, 0, rows_y, rows_z, (change,))
    changes = scattered(
        lambda k: lax.dynamic_slice_in_dim(change, k * block, block, 1), "ch"
    )
    rows_one = lax.all_gather(near_one, SPLIT, axis=0)
    pre_two, act_two, near_two = conv_layer(
        act_one, conv_w, 1, rows_y, rows_z, (rows_one, *changes)
    )
    rows_two = lax.all_gather(near_two, SPLIT, axis=0)

    mask = loss_mask.reshape(-1, 1).astype(FLOAT)
    slots_one = spread_slots(rows_one, conv_rows, rows_y, rows_z)
    parts = rotations(act_two, "ch")
    parts[-1] = after(parts[-1], slots_one)
    top, d_pred, sums, back, *pieces = predict(parts, changes, dec_w, mask, channels)

    def sent(pieces):
        return [shift(piece, "ch", by + 1) for by, piece in enumerate(pieces)]

    grad_dec = lax.dot_general(top, d_pred, (((0,), (0,)), ((), ())), preferred_element_type=FLOAT)
    keep, send = halves(grad_dec.astype(HALF).reshape(-1, dec_rows, block), 1)
    pieces = sent(pieces)
    pieces[-1] = after(pieces[-1], send)
    d_act_two, d_pre_two = step_back(back, pieces, pre_two, sums)
    slots_two = spread_slots(rows_two, conv_rows, rows_y, rows_z)
    errors_two = lax.all_gather(d_pre_two, SPLIT, axis=0)
    back, *pieces = conv_back(errors_two, conv_w, 1, rows_y, rows_z, count)
    _, d_pre_one = step_back(back, sent(pieces), pre_one, d_act_two)
    errors_one = lax.all_gather(d_pre_one, SPLIT, axis=0)

    grad_dec = halved(keep, send, (back, d_pre_one, errors_one))
    states = (conv_w, conv_m, conv_v)
    dec = (grad_dec, dec_w, dec_m, dec_v)
    two_shard, m_next, v_next, loss = kernel_step(
        slots_two, errors_two, errors_two, states, 1, (), (), rows_y, rows_z
    )
    one_shard, m_next, v_next, _, dec_m_next, dec_v_next = kernel_step(
        slots_one, errors_one, errors_two, states, 0, (m_next, v_next), dec, rows_y, rows_z
    )
    conv_next = settle(lax.all_gather(two_shard, SPLIT, axis=0), conv_w.shape, 1)
    pieces, last = cube_pieces(one_shard, conv_next)
    conv_next, dec_next = settle_pieces(with_partner(pieces), 0, conv_next, dec_w.shape, ())
    if last:
        last = [(mask, first, after(piece, conv_next)) for mask, first, piece in last]
        conv_next, dec_next = settle_pieces(
            with_partner(last), 0, conv_next, dec_w.shape, (dec_next,)
        )
    return (
        state,
        loss[0, 0],
        conv_next,
        dec_next,
        m_next,
        v_next,
        dec_m_next,
        dec_v_next,
    )


def solution(mesh):
    return jax.shard_map(
        body,
        mesh=mesh,
        in_specs=(
            P(None, ("grp", "sp"), "ch", None),
            P(None, "ch"),
            P(None, None, None, "ch"),
            P(None, "ch"),
            P(None, None, ("grp", "sp"), "ch"),
            P(None, None, ("grp", "sp"), "ch"),
            P(("grp", "sp"), "ch"),
            P(("grp", "sp"), "ch"),
            P(("grp", "sp"), None, None),
        ),
        out_specs=(
            P(None, ("grp", "sp"), "ch", None),
            P(),
            P(None, None, None, "ch"),
            P(None, "ch"),
            P(None, None, ("grp", "sp"), "ch"),
            P(None, None, ("grp", "sp"), "ch"),
            P(("grp", "sp"), "ch"),
            P(("grp", "sp"), "ch"),
        ),
        check_vma=False,
    )
```

```python
import jax
import jax.numpy as jnp
from jax import lax
from jax.experimental import pallas as pl
from jax.experimental.pallas import tpu as pltpu
from jax.sharding import PartitionSpec as P

PATCH = 8
FLOW_STEPS = 2
OUT = 2048
SPLIT = ("grp", "sp")


time_step = 0.1
viscosity = 0.2
beta_one = 0.9
beta_two = 0.95
learn_rate = 0.001
adam_eps = 1e-08
bias_one = 0.9999734386011124
bias_two = 0.994079470779666


def shift(block, axis, by):
    count = lax.axis_size(axis)
    return lax.ppermute(block, axis, [(i, (i + by) % count) for i in range(count)])


def with_halo(block, sides, width, hold):
    for axis, dim in sides:
        low = lax.slice_in_dim(block, block.shape[dim] - width, None, axis=dim)
        high = lax.slice_in_dim(block, 0, width, axis=dim)
        low, high, hold = lax.optimization_barrier((low, high, hold))
        low, high = shift(low, axis, 1), shift(high, axis, -1)
        block = jnp.concatenate([low, block, high], axis=dim)
    return block


def advance(padded):
    center = padded[:, 1:-1, 1:-1]
    east = padded[:, 2:, 1:-1]
    west = padded[:, :-2, 1:-1]
    north = padded[:, 1:-1, 2:]
    south = padded[:, 1:-1, :-2]
    upper = jnp.roll(center, -1, 3)
    lower = jnp.roll(center, 1, 3)
    laplace = east + west + north + south + upper + lower - 6.0 * center
    carried = (
        center[0:1] * (east - west) * 0.5
        + center[1:2] * (north - south) * 0.5
        + center[2:3] * (upper - lower) * 0.5
    )
    return center + time_step * (viscosity * laplace - carried)


def rotations(block, axis):
    return [block] + [shift(block, axis, by) for by in range(1, lax.axis_size(axis))]


def scattered(pieces_of, axis):
    count, own = lax.axis_size(axis), lax.axis_index(axis)
    parts = [pieces_of(own)]
    for by in range(1, count):
        parts.append(shift(pieces_of((own + by) % count), axis, by))
    return parts


BIG = pltpu.CompilerParams(vmem_limit_bytes=48 * 1024 * 1024)
FULL = pltpu.CompilerParams(vmem_limit_bytes=60 * 1024 * 1024)
FLOAT = jnp.float32
HALF = jnp.bfloat16


def like(shape, dtype):
    return jax.ShapeDtypeStruct(shape, dtype)


def whole_spec(shape):
    return pl.BlockSpec(shape, lambda *_: (0,) * len(shape))


def turn(block, by, groups):
    rows = block.shape[0] // groups
    cube = block.astype(FLOAT).reshape(groups, rows, block.shape[1])
    return pltpu.roll(cube, by % rows, 1).reshape(block.shape)


def to_patches(field):
    fields, depth, span, length = field.shape
    high, long = span // PATCH, length // PATCH
    flat = PATCH * PATCH
    cells = flat * PATCH

    def kernel(field_ref, out_ref):
        row = lax.broadcasted_iota(jnp.int32, (length, length), 0)
        col = lax.broadcasted_iota(jnp.int32, (length, length), 1)
        pick = (col == (row % long) * PATCH + row // long).astype(HALF)
        row = lax.broadcasted_iota(jnp.int32, (flat, cells), 0)
        col = lax.broadcasted_iota(jnp.int32, (flat, cells), 1)
        inside, deep = row == col // PATCH, col % PATCH
        grids = []
        for part in range(high):
            for index in range(fields):
                brick = field_ref[index, :, part * PATCH : (part + 1) * PATCH, :]
                brick = brick.reshape(flat, length).astype(HALF)
                grids.append(
                    lax.dot_general(
                        pick, brick, (((1,), (1,)), ((), ())), preferred_element_type=FLOAT
                    ).astype(HALF)
                )
        total = jnp.zeros((high * fields * long, cells), FLOAT)
        for step in range(PATCH):
            rows = jnp.concatenate(
                [grid[step * long : (step + 1) * long] for grid in grids], axis=0
            )
            place = (inside & (deep == step)).astype(HALF)
            total = total + jnp.dot(rows, place, preferred_element_type=FLOAT)
        for part in range(high):
            for index in range(fields):
                at = (part * fields + index) * long
                out_ref[
                    part * long : (part + 1) * long, index * cells : (index + 1) * cells
                ] = total[at : at + long].astype(HALF)

    return pl.pallas_call(
        kernel, out_shape=like((high * long, fields * cells), HALF), compiler_params=BIG
    )(field)


def axis_word(axis):
    return lax.axis_index(axis).astype(jnp.int32).reshape(1)


def after(value, *others):
    return lax.optimization_barrier((value, others))[0]


def ring_pieces(block, axis):
    count, rows = lax.axis_size(axis), block.shape[0]
    pieces, up, down = [(0, 0, block)], block, block
    for by in range(1, (count + 1) // 2):
        up, down = shift(up, axis, 1), shift(down, axis, -1)
        pieces += [(by, 0, up), (count - by, 0, down)]
    if count % 2 == 0:
        half = rows // 2
        pieces.append((count // 2, 0, shift(up[:half], axis, 1)))
        pieces.append((count // 2, half, shift(down[half:], axis, -1)))
    return pieces


def embed(pieces, rows, weight):
    count, cols = lax.axis_size("ch"), weight.shape[1]
    marks = [(by, first, piece.shape[0]) for by, first, piece in pieces]

    def kernel(own_ref, *refs):
        weight_ref, out_ref = refs[-2:]
        for (by, first, long), piece_ref in zip(marks, refs):
            at = lax.rem(own_ref[0] - by + count, count) * rows + first
            out_ref[pl.ds(pl.multiple_of(at, long), long), :] = jnp.dot(
                piece_ref[...], weight_ref[...], preferred_element_type=FLOAT
            ).astype(HALF)

    arrays = [piece for _, _, piece in pieces] + [weight]
    return pl.pallas_call(
        kernel,
        grid=(1,),
        out_shape=like((count * rows, cols), HALF),
        in_specs=[pl.BlockSpec(memory_space=pltpu.SMEM)] + [whole_spec(a.shape) for a in arrays],
        out_specs=whole_spec((count * rows, cols)),
        compiler_params=BIG,
    )(axis_word("ch"), *arrays)


def fetch(taps_ref, layer, held, sems, pairs):
    copies = {}
    for slot, pair in enumerate(pairs):
        copies[pair] = pltpu.make_async_copy(
            taps_ref.at[layer, pl.ds(3 * pair, 3)], held.at[slot], sems.at[slot]
        )
        copies[pair].start()
    return copies


def conv_planes(sources, kernels, layer, rows_y, rows_z, planes, tail):
    count, rows, cols = sources[0].shape
    width = count * cols
    pairs = [3 * plane + down for plane in planes for down in range(3)]

    def kernel(own_ref, *refs):
        source_refs, taps_ref = refs[: len(planes)], refs[len(planes)]
        grids, held, sems = refs[-3:]
        copies = fetch(taps_ref, layer, held, sems, pairs)
        for plane, source in enumerate(source_refs):
            for by in range(count):
                place = lax.rem(own_ref[0] - by + count, count)
                at = pl.ds(pl.multiple_of(place * cols, cols), cols)
                grids[plane, rows_z : rows_z + rows, at] = source[by]
                grids[plane, :rows_z, at] = source[by, rows - rows_z :]
                grids[plane, rows_z + rows :, at] = source[by, :rows_z]
        total = None
        for slot, pair in enumerate(pairs):
            copies[pair].wait()
            left = grids[slot // 3, pl.ds((slot % 3) * rows_z, rows), :]
            right = jnp.concatenate([held[slot, index] for index in range(3)], axis=1)
            part = jnp.dot(left, right, preferred_element_type=FLOAT)
            total = part if total is None else total + part
        if not tail:
            refs[-4][...] = total
            return
        act_ref, other_ref, pre_ref, out_ref = refs[len(planes) + 1 : len(planes) + 5]
        total = total + other_ref[...]
        pre = (
            turn(total[:, :cols], 1, rows_y)
            + total[:, cols : 2 * cols]
            + turn(total[:, 2 * cols :], -1, rows_y)
        )
        pre_ref[...] = pre
        out_ref[...] = (act_ref[...].astype(FLOAT) + pre / (1.0 + jnp.exp(-pre))).astype(HALF)

    outs = [like((rows, 3 * cols), FLOAT)]
    if tail:
        outs = [like((rows, cols), FLOAT), like((rows, cols), HALF)]
    return pl.pallas_call(
        kernel,
        grid=(1,),
        out_shape=outs,
        in_specs=[pl.BlockSpec(memory_space=pltpu.SMEM)]
        + [whole_spec(source.shape) for source in sources]
        + [pl.BlockSpec(memory_space=pl.ANY)]
        + [whole_spec(array.shape) for array in tail],
        out_specs=[whole_spec(out.shape) for out in outs],
        scratch_shapes=[
            pltpu.VMEM((len(planes), rows + 2 * rows_z, width), HALF),
            pltpu.VMEM((len(pairs), 3, width, cols), HALF),
            pltpu.SemaphoreType.DMA((len(pairs),)),
        ],
        compiler_params=BIG,
    )(axis_word("ch"), *sources, kernels, *tail)


def conv_layer(act, kernels, layer, rows_y, rows_z, hold):
    near = jnp.stack(rotations(act, "ch"))
    below, above = shift(near, SPLIT, 1), shift(near, SPLIT, -1)
    (middle,) = conv_planes((near,), kernels, layer, rows_y, rows_z, (1,), ())
    below = after(below, middle, *hold)
    pre, out = conv_planes(
        (below, above), kernels, layer, rows_y, rows_z, (0, 2), (act, middle)
    )
    return (pre, out, near)


def split_up(value):
    high = value.astype(HALF)
    rest = value - high.astype(FLOAT)
    middle = rest.astype(HALF)
    return [high, middle, (rest - middle.astype(FLOAT)).astype(HALF)]


def give(own_ref, total, cols, count, first_ref, piece_refs):
    for by in range(count):
        place = lax.rem(own_ref[0] + by, count)
        part = total[:, pl.ds(pl.multiple_of(place * cols, cols), cols)]
        if by == 0:
            first_ref[...] = part
        else:
            piece_refs[by - 1][: part.shape[0]] = part.astype(HALF)


def conv_back(errors, kernels, layer, rows_y, rows_z, count):
    planes, _, cols = errors.shape
    rows, width = rows_y * rows_z, count * cols
    pairs = list(range(9))

    def kernel(own_ref, *refs):
        error_refs, taps_ref, first_ref = refs[:3], refs[3], refs[4]
        piece_refs, sides, held, sems, total = refs[5 : 4 + count], *refs[4 + count :]
        copies = fetch(taps_ref, layer, held, sems, pairs)
        for plane in range(3):
            source = error_refs[plane][0]
            wide = jnp.concatenate(
                [
                    turn(source, -1, rows_y).astype(HALF),
                    source,
                    turn(source, 1, rows_y).astype(HALF),
                ],
                axis=1,
            )
            sides[plane, rows_z : rows_z + rows] = wide
            sides[plane, :rows_z] = wide[rows - rows_z :]
            sides[plane, rows_z + rows :] = wide[:rows_z]
        value = None
        for pair in pairs:
            copies[pair].wait()
            left = sides[pair // 3, pl.ds((2 - pair % 3) * rows_z, rows), :]
            right = jnp.concatenate([held[pair, index] for index in range(3)], axis=1)
            part = lax.dot_general(
                left, right, (((1,), (1,)), ((), ())), preferred_element_type=FLOAT
            )
            value = part if value is None else value + part
        total[...] = value
        give(own_ref, total, cols, count, first_ref, piece_refs)

    def plane_spec(offset):
        return pl.BlockSpec(
            (1, rows, cols), lambda step, word: (lax.rem(word[1] + offset + planes, planes), 0, 0)
        )

    word = jnp.concatenate([axis_word("ch"), axis_word(SPLIT)])
    return pl.pallas_call(
        kernel,
        grid_spec=pltpu.PrefetchScalarGridSpec(
            num_scalar_prefetch=1,
            grid=(1,),
            in_specs=[
                plane_spec(1),
                plane_spec(0),
                plane_spec(-1),
                pl.BlockSpec(memory_space=pl.ANY),
            ],
            out_specs=[whole_spec((rows, cols))] * count,
            scratch_shapes=[
                pltpu.VMEM((3, rows + 2 * rows_z, 3 * cols), HALF),
                pltpu.VMEM((9, 3, width, cols), HALF),
                pltpu.SemaphoreType.DMA((9,)),
                pltpu.VMEM((rows, width), FLOAT),
            ],
        ),
        out_shape=[like((rows, cols), FLOAT)] + [like((rows, cols), HALF)] * (count - 1),
        compiler_params=BIG,
    )(word, errors, errors, errors, kernels)


def step_back(own, pieces, pre, extra):
    rows, cols = own.shape
    stats = extra.shape[0] != rows

    def kernel(own_ref, *refs):
        piece_refs, pre_ref, extra_ref = refs[: len(pieces)], refs[-4], refs[-3]
        error_ref, send_ref = refs[-2:]
        error = own_ref[...]
        for ref in piece_refs:
            error = error + ref[:rows].astype(FLOAT)
        if not stats:
            error = error + extra_ref[...]
        error_ref[...] = error
        send_ref[:rows] = (error * silu_slope(pre_ref[...])).astype(HALF)
        if stats:
            squares = extra_ref[:1]
            for ref in piece_refs:
                for term in range(3):
                    squares = squares + ref[rows + term : rows + term + 1].astype(FLOAT)
            marked = extra_ref[1:2]
            coarse = jnp.floor(marked / 128.0)
            terms = split_up(squares) + [coarse.astype(HALF), (marked - 128.0 * coarse).astype(HALF)]
            terms.append(jnp.zeros((11, cols), HALF))
            send_ref[rows:] = jnp.concatenate([term.astype(FLOAT) for term in terms]).astype(HALF)

    arrays = [own, *pieces, pre, extra]
    outs = [like((rows, cols), FLOAT), like((rows + 16 * stats, cols), HALF)]
    return pl.pallas_call(
        kernel,
        grid=(1,),
        in_specs=[whole_spec(array.shape) for array in arrays],
        out_specs=[whole_spec(out.shape) for out in outs],
        out_shape=outs,
        compiler_params=BIG,
    )(*arrays)


def predict(parts, changes, weight, mask, channels):
    count = len(parts)
    rows, cols = parts[0].shape
    short, block = changes[0].shape
    width = count * cols

    def kernel(own_ref, *refs):
        part_refs, change_refs = refs[:count], refs[count : 2 * count]
        weight_ref, mask_ref = refs[2 * count], refs[2 * count + 1]
        outs = refs[2 * count + 2 :]
        top_ref, error_ref, sums_ref, first_ref = outs[:4]
        piece_refs, held = outs[4 : 3 + count], outs[3 + count]
        for by in range(count):
            place = lax.rem(own_ref[0] - by + count, count)
            top_ref[:, pl.ds(pl.multiple_of(place * cols, cols), cols)] = part_refs[by][...]
            held[pl.ds(pl.multiple_of(place * short, short), short), :] = change_refs[by][...]
        pred = jnp.dot(top_ref[...], weight_ref[...], preferred_element_type=FLOAT)
        resid = held[...].astype(FLOAT) + pred
        mask = mask_ref[...]
        marked = mask * resid
        error = marked.astype(HALF)
        error_ref[...] = error
        squares = jnp.full((1, cols), jnp.sum(marked * resid), FLOAT)
        marks = jnp.full((1, cols), jnp.sum(mask), FLOAT)
        sums_ref[...] = jnp.concatenate([squares, marks, jnp.zeros((6, cols), FLOAT)])
        terms = [term.astype(FLOAT) for term in split_up(squares)]
        terms = jnp.concatenate(terms + [jnp.zeros((13, cols), FLOAT)]).astype(HALF)
        for piece_ref in piece_refs:
            piece_ref[rows:] = terms
        total = refs[-1]
        total[...] = lax.dot_general(
            error, weight_ref[...], (((1,), (1,)), ((), ())), preferred_element_type=FLOAT
        )
        give(own_ref, total, cols, count, first_ref, piece_refs)

    arrays = [*parts, *changes, weight, mask]
    outs = [
        like((rows, width), HALF),
        like((rows, block), HALF),
        like((8, cols), FLOAT),
        like((rows, cols), FLOAT),
    ] + [like((rows + 16, cols), HALF)] * (count - 1)
    return pl.pallas_call(
        kernel,
        grid=(1,),
        in_specs=[pl.BlockSpec(memory_space=pltpu.SMEM)] + [whole_spec(a.shape) for a in arrays],
        out_specs=[whole_spec(out.shape) for out in outs],
        out_shape=outs,
        scratch_shapes=[pltpu.VMEM((rows, block), HALF), pltpu.VMEM((rows, width), FLOAT)],
        compiler_params=BIG,
    )(axis_word("ch"), *arrays)


def spread_slots(every, rows, rows_y, rows_z):
    planes, count, points, lane = every.shape
    each = lane // rows

    def kernel(word_ref, every_ref, slots, held, sem):
        read = pltpu.make_async_copy(every_ref.at[:, word_ref[1]], held, sem)
        read.start()
        offset = lax.rem(word_ref[0] * rows, lane)
        lanes = lax.broadcasted_iota(jnp.int32, (points, lane), 1)
        read.wait()

        def prepare(plane, carry):
            own = held[plane].astype(FLOAT)
            for slot in range(each):
                moved = pltpu.roll(own, lax.rem(slot * rows - offset + lane, lane), 1)
                inside = (lanes >= slot * rows) & (lanes < (slot + 1) * rows)
                moved = jnp.where(inside, moved, 0.0).astype(HALF)
                slots[slot, plane, rows_z : rows_z + points] = moved
                slots[slot, plane, :rows_z] = moved[points - rows_z :]
                slots[slot, plane, rows_z + points :] = moved[:rows_z]
            return carry

        lax.fori_loop(0, planes, prepare, 0)

    shape = (each, planes, points + 2 * rows_z, lane)
    place = axis_word(SPLIT)
    word = jnp.concatenate([place, (axis_word("ch") - place * rows // lane + count) % count])
    return pl.pallas_call(
        kernel,
        grid=(1,),
        in_specs=[pl.BlockSpec(memory_space=pltpu.SMEM), pl.BlockSpec(memory_space=pltpu.HBM)],
        out_specs=whole_spec(shape),
        out_shape=like(shape, HALF),
        scratch_shapes=[pltpu.VMEM((planes, points, lane), HALF), pltpu.SemaphoreType.DMA],
        compiler_params=FULL,
    )(word, every)


def kernel_step(slots, errors, counted, states, layer, kept, dec, rows_y, rows_z):
    each, planes, _, lane = slots.shape
    points, cols = rows_y * rows_z, errors.shape[2]
    rows = states[1].shape[2]
    blocks = -(-9 // each)
    solo = 2 * bool(dec)
    more = dec[1].shape[1] // cols if dec else 0
    chunk = 9

    def kernel(word_ref, slots_ref, errors_ref, counted_ref, w_hbm, m_hbm, v_hbm, *refs):
        dec_refs = refs[: len(dec)]
        refs = refs[len(dec) + len(kept) :]
        new_w, m_out, v_out, loss_ref, *dec_outs = refs[: 4 + solo]
        w_ref, m_ref, v_ref, new_m, new_v, total, sems, out_sems = refs[4 + solo :]
        reads = [
            pltpu.make_async_copy(
                w_hbm.at[layer, :, pl.ds(pl.multiple_of(word_ref[0] * rows, rows), rows)],
                w_ref,
                sems.at[0],
            ),
            pltpu.make_async_copy(m_hbm.at[layer], m_ref, sems.at[1]),
            pltpu.make_async_copy(v_hbm.at[layer], v_ref, sems.at[2]),
        ]
        for read in reads:
            read.start()
        total[...] = jnp.zeros_like(total)

        def gather(plane, carry):
            left = []
            for block in range(blocks):
                value = None
                for slot in range(each):
                    pair = block * each + slot
                    if pair < 9:
                        source = lax.rem(plane + pair // 3 - 1 + planes, planes)
                        part = slots_ref[slot, source, pl.ds((pair % 3) * rows_z, points), :]
                        value = part if value is None else value + part
                left.append(value)
            left = jnp.concatenate(left, axis=1)
            error = errors_ref[plane, :points]
            right = jnp.concatenate(
                [
                    turn(error, -1, rows_y).astype(HALF),
                    error,
                    turn(error, 1, rows_y).astype(HALF),
                ],
                axis=1,
            )
            total[...] += lax.dot_general(
                left, right, (((0,), (0,)), ((), ())), preferred_element_type=FLOAT
            )
            return carry

        lax.fori_loop(0, planes, gather, 0)
        stats = jnp.sum(counted_ref[...].astype(FLOAT), axis=0)
        denom = jnp.maximum(128.0 * stats[3:4, :1] + stats[4:5, :1], 1.0) * OUT
        scale = 2.0 / denom
        squares = (stats[0:1, :1] + stats[1:2, :1]) + stats[2:3, :1]
        loss_ref[...] = jnp.broadcast_to(squares / denom, (8, 128))
        for read in reads:
            read.wait()
        writes = []
        for tap in range(27):
            at = (tap // 3) * rows
            grad = total[at : at + rows, (tap % 3) * cols : (tap % 3 + 1) * cols] * scale
            weight_next, moment_next, second_next = adam(w_ref[tap], m_ref[tap], v_ref[tap], grad)
            new_w[tap] = weight_next
            new_m[tap] = moment_next
            new_v[tap] = second_next
            if tap % chunk == chunk - 1:
                part = pl.ds(tap + 1 - chunk, chunk)
                for source, out, side in ((new_m, m_out, 0), (new_v, v_out, 1)):
                    writes.append(
                        pltpu.make_async_copy(
                            source.at[part],
                            out.at[layer, part],
                            out_sems.at[2 * (tap // chunk) + side],
                        )
                    )
                    writes[-1].start()
        if dec:
            grad_ref, dec_w_ref, dec_m_ref, dec_v_ref = dec_refs
            weight_next, moment_next, second_next = adam(
                dec_w_ref[...], dec_m_ref[...], dec_v_ref[...], grad_ref[...] * scale
            )
            dec_outs[0][...] = moment_next
            dec_outs[1][...] = second_next
            for index in range(more):
                new_w[27 + index] = weight_next[:, index * cols : (index + 1) * cols]
        for write in writes:
            write.wait()

    any_spec = pl.BlockSpec(memory_space=pl.ANY)
    hbm_spec = pl.BlockSpec(memory_space=pltpu.HBM)
    dec_specs = []
    if dec:
        flat = whole_spec(dec[2].shape)
        dec_specs = [flat, pl.BlockSpec(dec[2].shape, lambda step, word: (word[0], 0)), flat, flat]
    outs = [
        like((27 + more, rows, cols), HALF),
        like(states[1].shape, FLOAT),
        like(states[2].shape, FLOAT),
        like((8, 128), FLOAT),
    ] + [like(array.shape, FLOAT) for array in dec[2:]]
    first = 7 + len(dec)
    return pl.pallas_call(
        kernel,
        grid_spec=pltpu.PrefetchScalarGridSpec(
            num_scalar_prefetch=1,
            grid=(1,),
            in_specs=[
                whole_spec(slots.shape),
                whole_spec(errors.shape),
                pl.BlockSpec((planes, 16, cols), lambda step, word: (0, points // 16, 0)),
                hbm_spec,
                hbm_spec,
                hbm_spec,
            ]
            + dec_specs
            + [any_spec] * len(kept),
            out_specs=[
                whole_spec((27 + more, rows, cols)),
                any_spec,
                any_spec,
                whole_spec((8, 128)),
            ]
            + [whole_spec(array.shape) for array in dec[2:]],
            scratch_shapes=[
                pltpu.VMEM((27, rows, cols), HALF),
                pltpu.VMEM((27, rows, cols), FLOAT),
                pltpu.VMEM((27, rows, cols), FLOAT),
                pltpu.VMEM((27, rows, cols), FLOAT),
                pltpu.VMEM((27, rows, cols), FLOAT),
                pltpu.VMEM((blocks * lane, 3 * cols), FLOAT),
                pltpu.SemaphoreType.DMA((3,)),
                pltpu.SemaphoreType.DMA((2 * 27 // chunk,)),
            ],
        ),
        out_shape=outs,
        input_output_aliases={first: 1, first + 1: 2} if kept else {},
        compiler_params=FULL,
    )(axis_word(SPLIT), slots, errors, counted, *states, *dec, *kept)


def settle(gathered, shape, layer):
    count, taps, rows, cols = gathered.shape

    def kernel(from_ref, out_ref):
        out_ref[0] = from_ref[0]

    return pl.pallas_call(
        kernel,
        grid=(count,),
        in_specs=[pl.BlockSpec((1, taps, rows, cols), lambda step: (step, 0, 0, 0))],
        out_specs=pl.BlockSpec((1, taps, rows, cols), lambda step: (layer, 0, step, 0)),
        out_shape=like(shape, HALF),
        compiler_params=BIG,
    )(gathered)


def cross(block, mask):
    count = lax.axis_size(SPLIT)
    return lax.ppermute(block, SPLIT, [(i, i ^ mask) for i in range(count)])


def with_partner(pieces):
    return pieces + [(mask + 1, first, cross(piece, 1)) for mask, first, piece in pieces]


def cube_pieces(block, hold):
    count, long = lax.axis_size(SPLIT), block.shape[0]
    outer = [1 << bit for bit in range(1, (count - 1).bit_length())]
    pieces, last = [(0, 0, block)], []
    if len(outer) == 2:
        one, two = outer
        half = long // 2
        by_one, by_two = cross(block, one), cross(block, two)
        by_one, by_two, _ = lax.optimization_barrier((by_one, by_two, hold))
        pieces += [(one, 0, by_one), (two, 0, by_two)]
        last.append((one + two, 0, cross(by_two[:half], one)))
        last.append((one + two, half, cross(by_one[half:], two)))
    else:
        for bit in outer:
            pieces += [(mask + bit, first, cross(piece, bit)) for mask, first, piece in pieces]
    return pieces, last


def settle_pieces(pieces, layer, kept, dec_shape, dec_kept):
    marks = [(mask, first, piece.shape[0]) for mask, first, piece in pieces]
    count, taps = len(pieces), kept.shape[1]
    _, rows, cols = pieces[0][2].shape
    every = sum(1 + max(0, first + long - taps) for _, first, long in marks)

    def kernel(place_ref, *refs):
        out_ref, dec_ref, sems = refs[-3:]
        copies = []

        def copy(source, target):
            copies.append(pltpu.make_async_copy(source, target, sems.at[len(copies)]))
            copies[-1].start()

        for ref, (mask, first, long) in zip(refs, marks):
            at = pl.ds(pl.multiple_of((place_ref[0] ^ mask) * rows, rows), rows)
            own = min(long, taps - first)
            copy(ref.at[pl.ds(0, own)], out_ref.at[layer, pl.ds(first, own), at])
            for index in range(own, long):
                column = (first + index - taps) * cols
                copy(ref.at[index], dec_ref.at[at, pl.ds(column, cols)])
        for started in copies:
            started.wait()

    any_spec = pl.BlockSpec(memory_space=pl.ANY)
    return pl.pallas_call(
        kernel,
        grid=(1,),
        in_specs=[pl.BlockSpec(memory_space=pltpu.SMEM)]
        + [whole_spec(piece.shape) for _, _, piece in pieces]
        + [any_spec] * (1 + len(dec_kept)),
        out_specs=[any_spec, any_spec],
        out_shape=[like(kept.shape, HALF), like(dec_shape, HALF)],
        scratch_shapes=[pltpu.SemaphoreType.DMA((every,))],
        input_output_aliases={count + 1 + index: index for index in range(1 + len(dec_kept))},
        compiler_params=BIG,
    )(axis_word(SPLIT), *[piece for _, _, piece in pieces], kept, *dec_kept)


def halves(block, bit):
    pairs = block.reshape(block.shape[0] // 2, 2, *block.shape[1:])
    mine = (lax.axis_index(SPLIT) // bit) % 2
    keep = lax.dynamic_index_in_dim(pairs, mine, 1, keepdims=False)
    send = lax.dynamic_index_in_dim(pairs, 1 - mine, 1, keepdims=False)
    return keep, send.astype(HALF)


def halved(keep, send, holds):
    bit, turn_at = 1, 0
    while True:
        sent = after(cross(send, bit), holds[min(turn_at, len(holds) - 1)])
        block = keep.astype(FLOAT) + sent.astype(FLOAT)
        bit, turn_at = 2 * bit, turn_at + 1
        if bit == lax.axis_size(SPLIT):
            return block[0]
        keep, send = halves(block, bit)


def silu_slope(value):
    sig = jax.nn.sigmoid(value)
    return sig * (1.0 + value * (1.0 - sig))


def adam(weight, moment, second, grad):
    moment_next = beta_one * moment + (1.0 - beta_one) * grad
    second_next = beta_two * second + (1.0 - beta_two) * grad * grad
    weight_next = weight.astype(jnp.float32) - learn_rate * (moment_next / bias_one) / (
        jnp.sqrt(second_next / bias_two) + adam_eps
    )
    return (weight_next.astype(jnp.bfloat16), moment_next, second_next)


def body(flow, embed_w, conv_w, dec_w, conv_m, conv_v, dec_m, dec_v, loss_mask):
    rows_y = flow.shape[2] * lax.axis_size("ch") // PATCH
    rows_z = flow.shape[3] // PATCH
    width = conv_w.shape[2]
    channels = conv_w.shape[3]
    block = dec_w.shape[1]
    dec_rows = dec_m.shape[0]
    conv_rows = conv_m.shape[2]

    count = lax.axis_size("ch")
    patches = to_patches(flow)
    pieces = ring_pieces(patches, "ch")
    padded = with_halo(flow, ((SPLIT, 1), ("ch", 2)), FLOW_STEPS, patches)
    by, first, piece = pieces[-1]
    pieces[-1] = (by, first, after(piece, padded))
    embedded = embed(pieces, patches.shape[0], embed_w)

    state = padded
    for step in range(FLOW_STEPS):
        state = advance(state)
    change = to_patches(flow.astype(HALF).astype(FLOAT) - state)
    pre_one, act_one, near_one = conv_layer(embedded, conv_w, 0, rows_y, rows_z, (change,))
    changes = scattered(
        lambda k: lax.dynamic_slice_in_dim(change, k * block, block, 1), "ch"
    )
    rows_one = lax.all_gather(near_one, SPLIT, axis=0)
    pre_two, act_two, near_two = conv_layer(
        act_one, conv_w, 1, rows_y, rows_z, (rows_one, *changes)
    )
    rows_two = lax.all_gather(near_two, SPLIT, axis=0)

    mask = loss_mask.reshape(-1, 1).astype(FLOAT)
    slots_one = spread_slots(rows_one, conv_rows, rows_y, rows_z)
    parts = rotations(act_two, "ch")
    parts[-1] = after(parts[-1], slots_one)
    top, d_pred, sums, back, *pieces = predict(parts, changes, dec_w, mask, channels)

    def sent(pieces):
        return [shift(piece, "ch", by + 1) for by, piece in enumerate(pieces)]

    grad_dec = lax.dot_general(top, d_pred, (((0,), (0,)), ((), ())), preferred_element_type=FLOAT)
    keep, send = halves(grad_dec.astype(HALF).reshape(-1, dec_rows, block), 1)
    pieces = sent(pieces)
    pieces[-1] = after(pieces[-1], send)
    d_act_two, d_pre_two = step_back(back, pieces, pre_two, sums)
    slots_two = spread_slots(rows_two, conv_rows, rows_y, rows_z)
    errors_two = lax.all_gather(d_pre_two, SPLIT, axis=0)
    back, *pieces = conv_back(errors_two, conv_w, 1, rows_y, rows_z, count)
    _, d_pre_one = step_back(back, sent(pieces), pre_one, d_act_two)
    errors_one = lax.all_gather(d_pre_one, SPLIT, axis=0)

    grad_dec = halved(keep, send, (back, d_pre_one, errors_one))
    states = (conv_w, conv_m, conv_v)
    dec = (grad_dec, dec_w, dec_m, dec_v)
    two_shard, m_next, v_next, loss = kernel_step(
        slots_two, errors_two, errors_two, states, 1, (), (), rows_y, rows_z
    )
    one_shard, m_next, v_next, _, dec_m_next, dec_v_next = kernel_step(
        slots_one, errors_one, errors_two, states, 0, (m_next, v_next), dec, rows_y, rows_z
    )
    conv_next = settle(lax.all_gather(two_shard, SPLIT, axis=0), conv_w.shape, 1)
    pieces, last = cube_pieces(one_shard, conv_next)
    conv_next, dec_next = settle_pieces(with_partner(pieces), 0, conv_next, dec_w.shape, ())
    if last:
        last = [(mask, first, after(piece, conv_next)) for mask, first, piece in last]
        conv_next, dec_next = settle_pieces(
            with_partner(last), 0, conv_next, dec_w.shape, (dec_next,)
        )
    return (
        state,
        loss[0, 0],
        conv_next,
        dec_next,
        m_next,
        v_next,
        dec_m_next,
        dec_v_next,
    )


def solution(mesh):
    return jax.shard_map(
        body,
        mesh=mesh,
        in_specs=(
            P(None, ("grp", "sp"), "ch", None),
            P(None, "ch"),
            P(None, None, None, "ch"),
            P(None, "ch"),
            P(None, None, ("grp", "sp"), "ch"),
            P(None, None, ("grp", "sp"), "ch"),
            P(("grp", "sp"), "ch"),
            P(("grp", "sp"), "ch"),
            P(("grp", "sp"), None, None),
        ),
        out_specs=(
            P(None, ("grp", "sp"), "ch", None),
            P(),
            P(None, None, None, "ch"),
            P(None, "ch"),
            P(None, None, ("grp", "sp"), "ch"),
            P(None, None, ("grp", "sp"), "ch"),
            P(("grp", "sp"), "ch"),
            P(("grp", "sp"), "ch"),
        ),
        check_vma=False,
    )
```

```python
import jax
import jax.numpy as jnp
from jax import lax
from jax.experimental import pallas as pl
from jax.experimental.pallas import tpu as pltpu
from jax.sharding import PartitionSpec as P

PATCH = 8
FLOW_STEPS = 2
OUT = 2048
SPLIT = ("grp", "sp")


time_step = 0.1
viscosity = 0.2
beta_one = 0.9
beta_two = 0.95
learn_rate = 0.001
adam_eps = 1e-08
bias_one = 0.9999734386011124
bias_two = 0.994079470779666


def shift(block, axis, by):
    count = lax.axis_size(axis)
    return lax.ppermute(block, axis, [(i, (i + by) % count) for i in range(count)])


def with_halo(block, sides, width, hold):
    for axis, dim in sides:
        low = lax.slice_in_dim(block, block.shape[dim] - width, None, axis=dim)
        high = lax.slice_in_dim(block, 0, width, axis=dim)
        low, high, hold = lax.optimization_barrier((low, high, hold))
        low, high = shift(low, axis, 1), shift(high, axis, -1)
        block = jnp.concatenate([low, block, high], axis=dim)
    return block


def advance(padded):
    center = padded[:, 1:-1, 1:-1]
    east = padded[:, 2:, 1:-1]
    west = padded[:, :-2, 1:-1]
    north = padded[:, 1:-1, 2:]
    south = padded[:, 1:-1, :-2]
    upper = jnp.roll(center, -1, 3)
    lower = jnp.roll(center, 1, 3)
    laplace = east + west + north + south + upper + lower - 6.0 * center
    carried = (
        center[0:1] * (east - west) * 0.5
        + center[1:2] * (north - south) * 0.5
        + center[2:3] * (upper - lower) * 0.5
    )
    return center + time_step * (viscosity * laplace - carried)


def rotations(block, axis):
    return [block] + [shift(block, axis, by) for by in range(1, lax.axis_size(axis))]


def scattered(pieces_of, axis):
    count, own = lax.axis_size(axis), lax.axis_index(axis)
    parts = [pieces_of(own)]
    for by in range(1, count):
        parts.append(shift(pieces_of((own + by) % count), axis, by))
    return parts


BIG = pltpu.CompilerParams(vmem_limit_bytes=48 * 1024 * 1024)
FULL = pltpu.CompilerParams(vmem_limit_bytes=60 * 1024 * 1024)
FLOAT = jnp.float32
HALF = jnp.bfloat16


def like(shape, dtype):
    return jax.ShapeDtypeStruct(shape, dtype)


def whole_spec(shape):
    return pl.BlockSpec(shape, lambda *_: (0,) * len(shape))


def turn(block, by, groups):
    rows = block.shape[0] // groups
    cube = block.astype(FLOAT).reshape(groups, rows, block.shape[1])
    return pltpu.roll(cube, by % rows, 1).reshape(block.shape)


def to_patches(field):
    fields, depth, span, length = field.shape
    high, long = span // PATCH, length // PATCH
    flat = PATCH * PATCH
    cells = flat * PATCH

    def kernel(field_ref, out_ref):
        row = lax.broadcasted_iota(jnp.int32, (length, length), 0)
        col = lax.broadcasted_iota(jnp.int32, (length, length), 1)
        pick = (col == (row % long) * PATCH + row // long).astype(HALF)
        row = lax.broadcasted_iota(jnp.int32, (flat, cells), 0)
        col = lax.broadcasted_iota(jnp.int32, (flat, cells), 1)
        inside, deep = row == col // PATCH, col % PATCH
        grids = []
        for part in range(high):
            for index in range(fields):
                brick = field_ref[index, :, part * PATCH : (part + 1) * PATCH, :]
                brick = brick.reshape(flat, length).astype(HALF)
                grids.append(
                    lax.dot_general(
                        pick, brick, (((1,), (1,)), ((), ())), preferred_element_type=FLOAT
                    ).astype(HALF)
                )
        total = jnp.zeros((high * fields * long, cells), FLOAT)
        for step in range(PATCH):
            rows = jnp.concatenate(
                [grid[step * long : (step + 1) * long] for grid in grids], axis=0
            )
            place = (inside & (deep == step)).astype(HALF)
            total = total + jnp.dot(rows, place, preferred_element_type=FLOAT)
        for part in range(high):
            for index in range(fields):
                at = (part * fields + index) * long
                out_ref[
                    part * long : (part + 1) * long, index * cells : (index + 1) * cells
                ] = total[at : at + long].astype(HALF)

    return pl.pallas_call(
        kernel, out_shape=like((high * long, fields * cells), HALF), compiler_params=BIG
    )(field)


def axis_word(axis):
    return lax.axis_index(axis).astype(jnp.int32).reshape(1)


def after(value, *others):
    return lax.optimization_barrier((value, others))[0]


def ring_pieces(block, axis):
    count, rows = lax.axis_size(axis), block.shape[0]
    pieces, up, down = [(0, 0, block)], block, block
    for by in range(1, (count + 1) // 2):
        up, down = shift(up, axis, 1), shift(down, axis, -1)
        pieces += [(by, 0, up), (count - by, 0, down)]
    if count % 2 == 0:
        half = rows // 2
        pieces.append((count // 2, 0, shift(up[:half], axis, 1)))
        pieces.append((count // 2, half, shift(down[half:], axis, -1)))
    return pieces


def embed(pieces, rows, weight):
    count, cols = lax.axis_size("ch"), weight.shape[1]
    marks = [(by, first, piece.shape[0]) for by, first, piece in pieces]

    def kernel(own_ref, *refs):
        weight_ref, out_ref = refs[-2:]
        for (by, first, long), piece_ref in zip(marks, refs):
            at = lax.rem(own_ref[0] - by + count, count) * rows + first
            out_ref[pl.ds(pl.multiple_of(at, long), long), :] = jnp.dot(
                piece_ref[...], weight_ref[...], preferred_element_type=FLOAT
            ).astype(HALF)

    arrays = [piece for _, _, piece in pieces] + [weight]
    return pl.pallas_call(
        kernel,
        grid=(1,),
        out_shape=like((count * rows, cols), HALF),
        in_specs=[pl.BlockSpec(memory_space=pltpu.SMEM)] + [whole_spec(a.shape) for a in arrays],
        out_specs=whole_spec((count * rows, cols)),
        compiler_params=BIG,
    )(axis_word("ch"), *arrays)


def fetch(taps_ref, layer, held, sems, pairs):
    copies = {}
    for slot, pair in enumerate(pairs):
        copies[pair] = pltpu.make_async_copy(
            taps_ref.at[layer, pl.ds(3 * pair, 3)], held.at[slot], sems.at[slot]
        )
        copies[pair].start()
    return copies


def conv_planes(sources, kernels, layer, rows_y, rows_z, planes, tail):
    count, rows, cols = sources[0].shape
    width = count * cols
    pairs = [3 * plane + down for plane in planes for down in range(3)]

    def kernel(own_ref, *refs):
        source_refs, taps_ref = refs[: len(planes)], refs[len(planes)]
        grids, held, sems = refs[-3:]
        copies = fetch(taps_ref, layer, held, sems, pairs)
        for plane, source in enumerate(source_refs):
            for by in range(count):
                place = lax.rem(own_ref[0] - by + count, count)
                at = pl.ds(pl.multiple_of(place * cols, cols), cols)
                grids[plane, rows_z : rows_z + rows, at] = source[by]
                grids[plane, :rows_z, at] = source[by, rows - rows_z :]
                grids[plane, rows_z + rows :, at] = source[by, :rows_z]
        total = None
        for slot, pair in enumerate(pairs):
            copies[pair].wait()
            left = grids[slot // 3, pl.ds((slot % 3) * rows_z, rows), :]
            right = jnp.concatenate([held[slot, index] for index in range(3)], axis=1)
            part = jnp.dot(left, right, preferred_element_type=FLOAT)
            total = part if total is None else total + part
        if not tail:
            refs[-4][...] = total
            return
        act_ref, other_ref, pre_ref, out_ref = refs[len(planes) + 1 : len(planes) + 5]
        total = total + other_ref[...]
        pre = (
            turn(total[:, :cols], 1, rows_y)
            + total[:, cols : 2 * cols]
            + turn(total[:, 2 * cols :], -1, rows_y)
        )
        pre_ref[...] = pre
        out_ref[...] = (act_ref[...].astype(FLOAT) + pre / (1.0 + jnp.exp(-pre))).astype(HALF)

    outs = [like((rows, 3 * cols), FLOAT)]
    if tail:
        outs = [like((rows, cols), FLOAT), like((rows, cols), HALF)]
    return pl.pallas_call(
        kernel,
        grid=(1,),
        out_shape=outs,
        in_specs=[pl.BlockSpec(memory_space=pltpu.SMEM)]
        + [whole_spec(source.shape) for source in sources]
        + [pl.BlockSpec(memory_space=pl.ANY)]
        + [whole_spec(array.shape) for array in tail],
        out_specs=[whole_spec(out.shape) for out in outs],
        scratch_shapes=[
            pltpu.VMEM((len(planes), rows + 2 * rows_z, width), HALF),
            pltpu.VMEM((len(pairs), 3, width, cols), HALF),
            pltpu.SemaphoreType.DMA((len(pairs),)),
        ],
        compiler_params=BIG,
    )(axis_word("ch"), *sources, kernels, *tail)


def conv_layer(act, kernels, layer, rows_y, rows_z, hold):
    near = jnp.stack(rotations(act, "ch"))
    below, above = shift(near, SPLIT, 1), shift(near, SPLIT, -1)
    (middle,) = conv_planes((near,), kernels, layer, rows_y, rows_z, (1,), ())
    below = after(below, middle, *hold)
    pre, out = conv_planes(
        (below, above), kernels, layer, rows_y, rows_z, (0, 2), (act, middle)
    )
    return (pre, out, near)


def split_up(value):
    high = value.astype(HALF)
    rest = value - high.astype(FLOAT)
    middle = rest.astype(HALF)
    return [high, middle, (rest - middle.astype(FLOAT)).astype(HALF)]


def give(own_ref, total, cols, count, first_ref, piece_refs):
    for by in range(count):
        place = lax.rem(own_ref[0] + by, count)
        part = total[:, pl.ds(pl.multiple_of(place * cols, cols), cols)]
        if by == 0:
            first_ref[...] = part
        else:
            piece_refs[by - 1][: part.shape[0]] = part.astype(HALF)


def conv_back(errors, kernels, layer, rows_y, rows_z, count):
    planes, _, cols = errors.shape
    rows, width = rows_y * rows_z, count * cols
    pairs = list(range(9))

    def kernel(own_ref, *refs):
        error_refs, taps_ref, first_ref = refs[:3], refs[3], refs[4]
        piece_refs, sides, held, sems, total = refs[5 : 4 + count], *refs[4 + count :]
        copies = fetch(taps_ref, layer, held, sems, pairs)
        for plane in range(3):
            source = error_refs[plane][0]
            wide = jnp.concatenate(
                [
                    turn(source, -1, rows_y).astype(HALF),
                    source,
                    turn(source, 1, rows_y).astype(HALF),
                ],
                axis=1,
            )
            sides[plane, rows_z : rows_z + rows] = wide
            sides[plane, :rows_z] = wide[rows - rows_z :]
            sides[plane, rows_z + rows :] = wide[:rows_z]
        value = None
        for pair in pairs:
            copies[pair].wait()
            left = sides[pair // 3, pl.ds((2 - pair % 3) * rows_z, rows), :]
            right = jnp.concatenate([held[pair, index] for index in range(3)], axis=1)
            part = lax.dot_general(
                left, right, (((1,), (1,)), ((), ())), preferred_element_type=FLOAT
            )
            value = part if value is None else value + part
        total[...] = value
        give(own_ref, total, cols, count, first_ref, piece_refs)

    def plane_spec(offset):
        return pl.BlockSpec(
            (1, rows, cols), lambda step, word: (lax.rem(word[1] + offset + planes, planes), 0, 0)
        )

    word = jnp.concatenate([axis_word("ch"), axis_word(SPLIT)])
    return pl.pallas_call(
        kernel,
        grid_spec=pltpu.PrefetchScalarGridSpec(
            num_scalar_prefetch=1,
            grid=(1,),
            in_specs=[
                plane_spec(1),
                plane_spec(0),
                plane_spec(-1),
                pl.BlockSpec(memory_space=pl.ANY),
            ],
            out_specs=[whole_spec((rows, cols))] * count,
            scratch_shapes=[
                pltpu.VMEM((3, rows + 2 * rows_z, 3 * cols), HALF),
                pltpu.VMEM((9, 3, width, cols), HALF),
                pltpu.SemaphoreType.DMA((9,)),
                pltpu.VMEM((rows, width), FLOAT),
            ],
        ),
        out_shape=[like((rows, cols), FLOAT)] + [like((rows, cols), HALF)] * (count - 1),
        compiler_params=BIG,
    )(word, errors, errors, errors, kernels)


def step_back(own, pieces, pre, extra):
    rows, cols = own.shape
    stats = extra.shape[0] != rows

    def kernel(own_ref, *refs):
        piece_refs, pre_ref, extra_ref = refs[: len(pieces)], refs[-4], refs[-3]
        error_ref, send_ref = refs[-2:]
        error = own_ref[...]
        for ref in piece_refs:
            error = error + ref[:rows].astype(FLOAT)
        if not stats:
            error = error + extra_ref[...]
        error_ref[...] = error
        send_ref[:rows] = (error * silu_slope(pre_ref[...])).astype(HALF)
        if stats:
            squares = extra_ref[:1]
            for ref in piece_refs:
                for term in range(3):
                    squares = squares + ref[rows + term : rows + term + 1].astype(FLOAT)
            marked = extra_ref[1:2]
            coarse = jnp.floor(marked / 128.0)
            terms = split_up(squares) + [coarse.astype(HALF), (marked - 128.0 * coarse).astype(HALF)]
            terms.append(jnp.zeros((11, cols), HALF))
            send_ref[rows:] = jnp.concatenate([term.astype(FLOAT) for term in terms]).astype(HALF)

    arrays = [own, *pieces, pre, extra]
    outs = [like((rows, cols), FLOAT), like((rows + 16 * stats, cols), HALF)]
    return pl.pallas_call(
        kernel,
        grid=(1,),
        in_specs=[whole_spec(array.shape) for array in arrays],
        out_specs=[whole_spec(out.shape) for out in outs],
        out_shape=outs,
        compiler_params=BIG,
    )(*arrays)


def predict(parts, changes, weight, mask, channels):
    count = len(parts)
    rows, cols = parts[0].shape
    short, block = changes[0].shape
    width = count * cols

    def kernel(own_ref, *refs):
        part_refs, change_refs = refs[:count], refs[count : 2 * count]
        weight_ref, mask_ref = refs[2 * count], refs[2 * count + 1]
        outs = refs[2 * count + 2 :]
        top_ref, error_ref, sums_ref, first_ref = outs[:4]
        piece_refs, held = outs[4 : 3 + count], outs[3 + count]
        for by in range(count):
            place = lax.rem(own_ref[0] - by + count, count)
            top_ref[:, pl.ds(pl.multiple_of(place * cols, cols), cols)] = part_refs[by][...]
            held[pl.ds(pl.multiple_of(place * short, short), short), :] = change_refs[by][...]
        pred = jnp.dot(top_ref[...], weight_ref[...], preferred_element_type=FLOAT)
        resid = held[...].astype(FLOAT) + pred
        mask = mask_ref[...]
        marked = mask * resid
        error = marked.astype(HALF)
        error_ref[...] = error
        squares = jnp.full((1, cols), jnp.sum(marked * resid), FLOAT)
        marks = jnp.full((1, cols), jnp.sum(mask), FLOAT)
        sums_ref[...] = jnp.concatenate([squares, marks, jnp.zeros((6, cols), FLOAT)])
        terms = [term.astype(FLOAT) for term in split_up(squares)]
        terms = jnp.concatenate(terms + [jnp.zeros((13, cols), FLOAT)]).astype(HALF)
        for piece_ref in piece_refs:
            piece_ref[rows:] = terms
        total = refs[-1]
        total[...] = lax.dot_general(
            error, weight_ref[...], (((1,), (1,)), ((), ())), preferred_element_type=FLOAT
        )
        give(own_ref, total, cols, count, first_ref, piece_refs)

    arrays = [*parts, *changes, weight, mask]
    outs = [
        like((rows, width), HALF),
        like((rows, block), HALF),
        like((8, cols), FLOAT),
        like((rows, cols), FLOAT),
    ] + [like((rows + 16, cols), HALF)] * (count - 1)
    return pl.pallas_call(
        kernel,
        grid=(1,),
        in_specs=[pl.BlockSpec(memory_space=pltpu.SMEM)] + [whole_spec(a.shape) for a in arrays],
        out_specs=[whole_spec(out.shape) for out in outs],
        out_shape=outs,
        scratch_shapes=[pltpu.VMEM((rows, block), HALF), pltpu.VMEM((rows, width), FLOAT)],
        compiler_params=BIG,
    )(axis_word("ch"), *arrays)


def fill_slots(word_ref, held, slots, rows, rows_z):
    each, planes, _, lane = slots.shape
    points = held.shape[1]
    offset = lax.rem(word_ref[0] * rows, lane)
    lanes = lax.broadcasted_iota(jnp.int32, (points, lane), 1)

    def prepare(plane, carry):
        own = held[plane].astype(FLOAT)
        for slot in range(each):
            moved = pltpu.roll(own, lax.rem(slot * rows - offset + lane, lane), 1)
            inside = (lanes >= slot * rows) & (lanes < (slot + 1) * rows)
            moved = jnp.where(inside, moved, 0.0).astype(HALF)
            slots[slot, plane, rows_z : rows_z + points] = moved
            slots[slot, plane, :rows_z] = moved[points - rows_z :]
            slots[slot, plane, rows_z + points :] = moved[:rows_z]
        return carry

    lax.fori_loop(0, planes, prepare, 0)


def spread_slots(every, rows, rows_y, rows_z):
    planes, count, points, lane = every.shape
    each = lane // rows

    def kernel(word_ref, every_ref, slots, held, sem):
        read = pltpu.make_async_copy(every_ref.at[:, word_ref[1]], held, sem)
        read.start()
        read.wait()
        fill_slots(word_ref, held, slots, rows, rows_z)

    shape = (each, planes, points + 2 * rows_z, lane)
    place = axis_word(SPLIT)
    word = jnp.concatenate([place, (axis_word("ch") - place * rows // lane + count) % count])
    return pl.pallas_call(
        kernel,
        grid=(1,),
        in_specs=[pl.BlockSpec(memory_space=pltpu.SMEM), pl.BlockSpec(memory_space=pltpu.HBM)],
        out_specs=whole_spec(shape),
        out_shape=like(shape, HALF),
        scratch_shapes=[pltpu.VMEM((planes, points, lane), HALF), pltpu.SemaphoreType.DMA],
        compiler_params=FULL,
    )(word, every)


def kernel_step(slots, errors, counted, states, layer, kept, dec, rows_y, rows_z):
    points, cols = rows_y * rows_z, errors.shape[2]
    rows = states[1].shape[2]
    raw = slots.shape[2] == points
    if raw:
        planes, _, _, lane = slots.shape
        each = lane // rows
    else:
        each, planes, _, lane = slots.shape
    blocks = -(-9 // each)
    solo = 2 * bool(dec)
    more = dec[1].shape[1] // cols if dec else 0
    chunk = 9

    def kernel(word_ref, slots_ref, errors_ref, counted_ref, w_hbm, m_hbm, v_hbm, *refs):
        dec_refs = refs[: len(dec)]
        refs = refs[len(dec) + len(kept) :]
        new_w, m_out, v_out, loss_ref, *dec_outs = refs[: 4 + solo]
        w_ref, m_ref, v_ref, new_m, new_v, total, sems, out_sems, *rest = refs[4 + solo :]
        if raw:
            first_read = pltpu.make_async_copy(slots_ref.at[:, word_ref[1]], rest[1], rest[2])
            first_read.start()
        reads = [
            pltpu.make_async_copy(
                w_hbm.at[layer, :, pl.ds(pl.multiple_of(word_ref[0] * rows, rows), rows)],
                w_ref,
                sems.at[0],
            ),
            pltpu.make_async_copy(m_hbm.at[layer], m_ref, sems.at[1]),
            pltpu.make_async_copy(v_hbm.at[layer], v_ref, sems.at[2]),
        ]
        for read in reads:
            read.start()
        total[...] = jnp.zeros_like(total)
        if raw:
            slots_ref = rest[0]
            first_read.wait()
            fill_slots(word_ref, rest[1], slots_ref, rows, rows_z)

        def gather(plane, carry):
            left = []
            for block in range(blocks):
                value = None
                for slot in range(each):
                    pair = block * each + slot
                    if pair < 9:
                        source = lax.rem(plane + pair // 3 - 1 + planes, planes)
                        part = slots_ref[slot, source, pl.ds((pair % 3) * rows_z, points), :]
                        value = part if value is None else value + part
                left.append(value)
            left = jnp.concatenate(left, axis=1)
            error = errors_ref[plane, :points]
            right = jnp.concatenate(
                [
                    turn(error, -1, rows_y).astype(HALF),
                    error,
                    turn(error, 1, rows_y).astype(HALF),
                ],
                axis=1,
            )
            total[...] += lax.dot_general(
                left, right, (((0,), (0,)), ((), ())), preferred_element_type=FLOAT
            )
            return carry

        lax.fori_loop(0, planes, gather, 0)
        stats = jnp.sum(counted_ref[...].astype(FLOAT), axis=0)
        denom = jnp.maximum(128.0 * stats[3:4, :1] + stats[4:5, :1], 1.0) * OUT
        scale = 2.0 / denom
        squares = (stats[0:1, :1] + stats[1:2, :1]) + stats[2:3, :1]
        loss_ref[...] = jnp.broadcast_to(squares / denom, (8, 128))
        for read in reads:
            read.wait()
        writes = []
        for tap in range(27):
            at = (tap // 3) * rows
            grad = total[at : at + rows, (tap % 3) * cols : (tap % 3 + 1) * cols] * scale
            weight_next, moment_next, second_next = adam(w_ref[tap], m_ref[tap], v_ref[tap], grad)
            new_w[tap] = weight_next
            new_m[tap] = moment_next
            new_v[tap] = second_next
            if tap % chunk == chunk - 1:
                part = pl.ds(tap + 1 - chunk, chunk)
                for source, out, side in ((new_m, m_out, 0), (new_v, v_out, 1)):
                    writes.append(
                        pltpu.make_async_copy(
                            source.at[part],
                            out.at[layer, part],
                            out_sems.at[2 * (tap // chunk) + side],
                        )
                    )
                    writes[-1].start()
        if dec:
            grad_ref, dec_w_ref, dec_m_ref, dec_v_ref = dec_refs
            weight_next, moment_next, second_next = adam(
                dec_w_ref[...], dec_m_ref[...], dec_v_ref[...], grad_ref[...] * scale
            )
            dec_outs[0][...] = moment_next
            dec_outs[1][...] = second_next
            for index in range(more):
                new_w[27 + index] = weight_next[:, index * cols : (index + 1) * cols]
        for write in writes:
            write.wait()

    any_spec = pl.BlockSpec(memory_space=pl.ANY)
    hbm_spec = pl.BlockSpec(memory_space=pltpu.HBM)
    place, count = axis_word(SPLIT), lax.axis_size("ch")
    word = jnp.concatenate([place, (axis_word("ch") - place * rows // lane + count) % count])
    raw_scratch = []
    if raw:
        raw_scratch = [
            pltpu.VMEM((each, planes, points + 2 * rows_z, lane), HALF),
            pltpu.VMEM((planes, points, lane), HALF),
            pltpu.SemaphoreType.DMA,
        ]
    dec_specs = []
    if dec:
        flat = whole_spec(dec[2].shape)
        dec_specs = [flat, pl.BlockSpec(dec[2].shape, lambda step, word: (word[0], 0)), flat, flat]
    outs = [
        like((27 + more, rows, cols), HALF),
        like(states[1].shape, FLOAT),
        like(states[2].shape, FLOAT),
        like((8, 128), FLOAT),
    ] + [like(array.shape, FLOAT) for array in dec[2:]]
    first = 7 + len(dec)
    return pl.pallas_call(
        kernel,
        grid_spec=pltpu.PrefetchScalarGridSpec(
            num_scalar_prefetch=1,
            grid=(1,),
            in_specs=[
                hbm_spec if raw else whole_spec(slots.shape),
                whole_spec(errors.shape),
                pl.BlockSpec((planes, 16, cols), lambda step, word: (0, points // 16, 0)),
                hbm_spec,
                hbm_spec,
                hbm_spec,
            ]
            + dec_specs
            + [any_spec] * len(kept),
            out_specs=[
                whole_spec((27 + more, rows, cols)),
                any_spec,
                any_spec,
                whole_spec((8, 128)),
            ]
            + [whole_spec(array.shape) for array in dec[2:]],
            scratch_shapes=[
                pltpu.VMEM((27, rows, cols), HALF),
                pltpu.VMEM((27, rows, cols), FLOAT),
                pltpu.VMEM((27, rows, cols), FLOAT),
                pltpu.VMEM((27, rows, cols), FLOAT),
                pltpu.VMEM((27, rows, cols), FLOAT),
                pltpu.VMEM((blocks * lane, 3 * cols), FLOAT),
                pltpu.SemaphoreType.DMA((3,)),
                pltpu.SemaphoreType.DMA((2 * 27 // chunk,)),
            ]
            + raw_scratch,
        ),
        out_shape=outs,
        input_output_aliases={first: 1, first + 1: 2} if kept else {},
        compiler_params=FULL,
    )(word, slots, errors, counted, *states, *dec, *kept)


def settle(gathered, shape, layer):
    count, taps, rows, cols = gathered.shape

    def kernel(from_ref, out_ref):
        out_ref[0] = from_ref[0]

    return pl.pallas_call(
        kernel,
        grid=(count,),
        in_specs=[pl.BlockSpec((1, taps, rows, cols), lambda step: (step, 0, 0, 0))],
        out_specs=pl.BlockSpec((1, taps, rows, cols), lambda step: (layer, 0, step, 0)),
        out_shape=like(shape, HALF),
        compiler_params=BIG,
    )(gathered)


def cross(block, mask):
    count = lax.axis_size(SPLIT)
    return lax.ppermute(block, SPLIT, [(i, i ^ mask) for i in range(count)])


def with_partner(pieces):
    return pieces + [(mask + 1, first, cross(piece, 1)) for mask, first, piece in pieces]


def cube_pieces(block, hold):
    count, long = lax.axis_size(SPLIT), block.shape[0]
    outer = [1 << bit for bit in range(1, (count - 1).bit_length())]
    pieces, last = [(0, 0, block)], []
    if len(outer) == 2:
        one, two = outer
        half = long // 2
        by_one, by_two = cross(block, one), cross(block, two)
        by_one, by_two, _ = lax.optimization_barrier((by_one, by_two, hold))
        pieces += [(one, 0, by_one), (two, 0, by_two)]
        last.append((one + two, 0, cross(by_two[:half], one)))
        last.append((one + two, half, cross(by_one[half:], two)))
    else:
        for bit in outer:
            pieces += [(mask + bit, first, cross(piece, bit)) for mask, first, piece in pieces]
    return pieces, last


def settle_pieces(pieces, layer, kept, dec_shape, dec_kept):
    marks = [(mask, first, piece.shape[0]) for mask, first, piece in pieces]
    count, taps = len(pieces), kept.shape[1]
    _, rows, cols = pieces[0][2].shape
    every = sum(1 + max(0, first + long - taps) for _, first, long in marks)

    def kernel(place_ref, *refs):
        out_ref, dec_ref, sems = refs[-3:]
        copies = []

        def copy(source, target):
            copies.append(pltpu.make_async_copy(source, target, sems.at[len(copies)]))
            copies[-1].start()

        for ref, (mask, first, long) in zip(refs, marks):
            at = pl.ds(pl.multiple_of((place_ref[0] ^ mask) * rows, rows), rows)
            own = min(long, taps - first)
            copy(ref.at[pl.ds(0, own)], out_ref.at[layer, pl.ds(first, own), at])
            for index in range(own, long):
                column = (first + index - taps) * cols
                copy(ref.at[index], dec_ref.at[at, pl.ds(column, cols)])
        for started in copies:
            started.wait()

    any_spec = pl.BlockSpec(memory_space=pl.ANY)
    return pl.pallas_call(
        kernel,
        grid=(1,),
        in_specs=[pl.BlockSpec(memory_space=pltpu.SMEM)]
        + [whole_spec(piece.shape) for _, _, piece in pieces]
        + [any_spec] * (1 + len(dec_kept)),
        out_specs=[any_spec, any_spec],
        out_shape=[like(kept.shape, HALF), like(dec_shape, HALF)],
        scratch_shapes=[pltpu.SemaphoreType.DMA((every,))],
        input_output_aliases={count + 1 + index: index for index in range(1 + len(dec_kept))},
        compiler_params=BIG,
    )(axis_word(SPLIT), *[piece for _, _, piece in pieces], kept, *dec_kept)


def halves(block, bit):
    pairs = block.reshape(block.shape[0] // 2, 2, *block.shape[1:])
    mine = (lax.axis_index(SPLIT) // bit) % 2
    keep = lax.dynamic_index_in_dim(pairs, mine, 1, keepdims=False)
    send = lax.dynamic_index_in_dim(pairs, 1 - mine, 1, keepdims=False)
    return keep, send.astype(HALF)


def halved(keep, send, holds):
    bit, turn_at = 1, 0
    while True:
        sent = after(cross(send, bit), holds[min(turn_at, len(holds) - 1)])
        block = keep.astype(FLOAT) + sent.astype(FLOAT)
        bit, turn_at = 2 * bit, turn_at + 1
        if bit == lax.axis_size(SPLIT):
            return block[0]
        keep, send = halves(block, bit)


def silu_slope(value):
    sig = jax.nn.sigmoid(value)
    return sig * (1.0 + value * (1.0 - sig))


def adam(weight, moment, second, grad):
    moment_next = beta_one * moment + (1.0 - beta_one) * grad
    second_next = beta_two * second + (1.0 - beta_two) * grad * grad
    weight_next = weight.astype(jnp.float32) - learn_rate * (moment_next / bias_one) / (
        jnp.sqrt(second_next / bias_two) + adam_eps
    )
    return (weight_next.astype(jnp.bfloat16), moment_next, second_next)


def body(flow, embed_w, conv_w, dec_w, conv_m, conv_v, dec_m, dec_v, loss_mask):
    rows_y = flow.shape[2] * lax.axis_size("ch") // PATCH
    rows_z = flow.shape[3] // PATCH
    width = conv_w.shape[2]
    channels = conv_w.shape[3]
    block = dec_w.shape[1]
    dec_rows = dec_m.shape[0]
    conv_rows = conv_m.shape[2]

    count = lax.axis_size("ch")
    patches = to_patches(flow)
    pieces = ring_pieces(patches, "ch")
    padded = with_halo(flow, ((SPLIT, 1), ("ch", 2)), FLOW_STEPS, patches)
    by, first, piece = pieces[-1]
    pieces[-1] = (by, first, after(piece, padded))
    embedded = embed(pieces, patches.shape[0], embed_w)

    state = padded
    for step in range(FLOW_STEPS):
        state = advance(state)
    change = to_patches(flow.astype(HALF).astype(FLOAT) - state)
    pre_one, act_one, near_one = conv_layer(embedded, conv_w, 0, rows_y, rows_z, (change,))
    changes = scattered(
        lambda k: lax.dynamic_slice_in_dim(change, k * block, block, 1), "ch"
    )
    rows_one = lax.all_gather(near_one, SPLIT, axis=0)
    pre_two, act_two, near_two = conv_layer(
        act_one, conv_w, 1, rows_y, rows_z, (rows_one, *changes)
    )
    rows_two = lax.all_gather(near_two, SPLIT, axis=0)

    mask = loss_mask.reshape(-1, 1).astype(FLOAT)
    slots_one = spread_slots(rows_one, conv_rows, rows_y, rows_z)
    parts = rotations(act_two, "ch")
    parts[-1] = after(parts[-1], slots_one)
    top, d_pred, sums, back, *pieces = predict(parts, changes, dec_w, mask, channels)

    def sent(pieces):
        return [shift(piece, "ch", by + 1) for by, piece in enumerate(pieces)]

    grad_dec = lax.dot_general(top, d_pred, (((0,), (0,)), ((), ())), preferred_element_type=FLOAT)
    keep, send = halves(grad_dec.astype(HALF).reshape(-1, dec_rows, block), 1)
    pieces = sent(pieces)
    pieces[-1] = after(pieces[-1], send)
    d_act_two, d_pre_two = step_back(back, pieces, pre_two, sums)
    errors_two = lax.all_gather(d_pre_two, SPLIT, axis=0)
    back, *pieces = conv_back(errors_two, conv_w, 1, rows_y, rows_z, count)
    _, d_pre_one = step_back(back, sent(pieces), pre_one, d_act_two)
    errors_one = lax.all_gather(d_pre_one, SPLIT, axis=0)

    grad_dec = halved(keep, send, (back, d_pre_one, errors_one))
    states = (conv_w, conv_m, conv_v)
    dec = (grad_dec, dec_w, dec_m, dec_v)
    two_shard, m_next, v_next, loss = kernel_step(
        rows_two, errors_two, errors_two, states, 1, (), (), rows_y, rows_z
    )
    one_shard, m_next, v_next, _, dec_m_next, dec_v_next = kernel_step(
        slots_one, errors_one, errors_two, states, 0, (m_next, v_next), dec, rows_y, rows_z
    )
    conv_next = settle(lax.all_gather(two_shard, SPLIT, axis=0), conv_w.shape, 1)
    pieces, last = cube_pieces(one_shard, conv_next)
    conv_next, dec_next = settle_pieces(with_partner(pieces), 0, conv_next, dec_w.shape, ())
    if last:
        last = [(mask, first, after(piece, conv_next)) for mask, first, piece in last]
        conv_next, dec_next = settle_pieces(
            with_partner(last), 0, conv_next, dec_w.shape, (dec_next,)
        )
    return (
        state,
        loss[0, 0],
        conv_next,
        dec_next,
        m_next,
        v_next,
        dec_m_next,
        dec_v_next,
    )


def solution(mesh):
    return jax.shard_map(
        body,
        mesh=mesh,
        in_specs=(
            P(None, ("grp", "sp"), "ch", None),
            P(None, "ch"),
            P(None, None, None, "ch"),
            P(None, "ch"),
            P(None, None, ("grp", "sp"), "ch"),
            P(None, None, ("grp", "sp"), "ch"),
            P(("grp", "sp"), "ch"),
            P(("grp", "sp"), "ch"),
            P(("grp", "sp"), None, None),
        ),
        out_specs=(
            P(None, ("grp", "sp"), "ch", None),
            P(),
            P(None, None, None, "ch"),
            P(None, "ch"),
            P(None, None, ("grp", "sp"), "ch"),
            P(None, None, ("grp", "sp"), "ch"),
            P(("grp", "sp"), "ch"),
            P(("grp", "sp"), "ch"),
        ),
        check_vma=False,
    )
```
